256 devices in a mesh: pop: 32 (over x, y, core), row: 8 (over z).
Axes of the slice: x: 4, y: 4, z: 8, core: 2. Of those that a mesh axis runs over, the one named last changes fastest.
Arguments:
- tokens: bfloat16 [1536, 16, 4096], P('pop'), may hold values from -6 to 6
- weight: bfloat16 [14336, 4096], P('row', 'pop'), may hold values from -0.09375 to 0.09375
- bank_in: bfloat16 [4096, 128], P('row'), may hold values from -0.09375 to 0.09375
- bank_out: bfloat16 [14336, 128], P('row'), may hold values from -6 to 6
- fitness: int32 [1536], P('pop'), may hold values from 0 to 767
- past_seeds: int32 [1536, 2, 8], P('pop'), may hold values from 0 to 127
- new_seeds: int32 [1536, 2, 8], P('pop'), may hold values from 0 to 127
Outputs:
- hidden: bfloat16 [1536, 16, 14336], P('pop', None, 'row')
- new_weight: bfloat16 [14336, 4096], P('row', 'pop')
The draws below stay inside these ranges and needn't reach their ends.
All inputs are finite; a program needn't handle non-finite values.
Results may differ from the reference program's by a relative error of at most 0.012.
Values may be sent and summed in bfloat16 or wider, within the bound.
A program may use at most 128 MiB of HBM per device.

```python
import jax
import jax.numpy as jnp
from jax import lax

D = 4096
FF = 14336
MEM_DEV = 48
TOK = 16
RANK = 8
BANK = 128
MEMBERS = 1536
N_POP = 32


def touch_ends(drawn, key, smallest, largest):
    place = [jax.random.randint(jax.random.fold_in(key, axis), (), 0, length) for axis, length in enumerate(drawn.shape)]
    longest = drawn.shape.index(max(drawn.shape))
    neighbour = place[:longest] + [(place[longest] + 1) % drawn.shape[longest]] + place[longest + 1:]
    return drawn.at[tuple(place)].set(smallest).at[tuple(neighbour)].set(largest)


def steps_of(rng, dims, shards, smallest, high):
    gain, own = 1.0, jax.random.fold_in(rng, 6)
    for axis_at, blocks in shards:
        steps = jnp.exp(jax.random.uniform(jax.random.fold_in(own, axis_at), (blocks,), jnp.float32, smallest / len(shards), high / len(shards)))
        gain = gain * jnp.repeat(steps, dims[axis_at] // blocks).reshape([-1 if axis == axis_at else 1 for axis in range(len(dims))])
    return gain


def scatter_about(rng, extent, spread, limit, pieces=(), held_as=jnp.bfloat16):
    entries = jax.random.normal(rng, extent, jnp.float32) * spread
    if len(pieces) > 0:
        entries = steps_of(rng, extent, pieces, -0.22, 0.18) * entries
    return jnp.clip(entries, min=-limit, max=limit).astype(held_as)


def setup_inputs(seed: int = 0) -> dict:
    key_list = jax.random.split(jax.random.key(seed), 8)
    return {
        "tokens": scatter_about(key_list[0], (MEMBERS, TOK, D), 1.0, 6.0, ((0, 32),)),
        "weight": scatter_about(key_list[1], (FF, D), D ** -0.5, 0.09375, ((0, 8), (1, 32))),
        "bank_in": scatter_about(key_list[2], (D, BANK), D ** -0.5, 0.09375, ((0, 8),)),
        "bank_out": scatter_about(key_list[3], (FF, BANK), 1.0, 6.0, ((0, 8),)),
        "fitness": touch_ends(jax.random.randint(key_list[4], (MEMBERS,), 0, MEMBERS // 2), jax.random.fold_in(key_list[4], 1), 0, (MEMBERS // 2) - 1).astype(jnp.int32),
        "past_seeds": touch_ends(jax.random.randint(key_list[5], (MEMBERS, 2, RANK), 0, BANK), jax.random.fold_in(key_list[5], 1), 0, BANK - 1).astype(jnp.int32),
        "new_seeds": touch_ends(jax.random.randint(key_list[6], (MEMBERS, 2, RANK), 0, BANK), jax.random.fold_in(key_list[6], 1), 0, BANK - 1).astype(jnp.int32),
    }


NOISE_SCALE = 0.1
STEP_SCALE = 0.03


def one_hots(seeds):
    levels = jnp.arange(BANK, dtype=jnp.int32)
    out_hits = (seeds[:, 0, :, None] == levels).astype(jnp.float32)
    in_hits = (seeds[:, 1, :, None] == levels).astype(jnp.float32)
    return out_hits, in_hits


def reference(tokens, weight, bank_in, bank_out, fitness, past_seeds, new_seeds):
    lower_count = jnp.sum((fitness[None, :] < fitness[:, None]).astype(jnp.float32), axis=1)
    equal_count = jnp.sum((fitness[None, :] == fitness[:, None]).astype(jnp.float32), axis=1)
    centered = (lower_count + 0.5 * (equal_count - 1.0)) / (MEMBERS - 1.0) - 0.5
    out_hits, in_hits = one_hots(past_seeds)
    coupling = STEP_SCALE * jnp.einsum("m,mki,mkj->ij", centered, out_hits, in_hits)
    left_part = jnp.dot(bank_out.astype(jnp.float32), coupling, precision=lax.Precision.HIGHEST)
    update = jnp.dot(left_part, bank_in.astype(jnp.float32).T, precision=lax.Precision.HIGHEST)
    new_weight = (weight.astype(jnp.float32) + update).astype(jnp.bfloat16)
    grouped_tokens = tokens.reshape(N_POP, MEM_DEV, TOK, D)
    grouped_seeds = new_seeds.reshape(N_POP, MEM_DEV, 2, RANK)

    def forward(packed):
        member_tokens, member_seeds = packed
        flat_tokens = member_tokens.reshape(MEM_DEV * TOK, D)
        base_part = lax.dot_general(flat_tokens, new_weight, (((1,), (1,)), ((), ())), preferred_element_type=jnp.float32)
        projected = jnp.dot(flat_tokens, bank_in, preferred_element_type=jnp.float32).reshape(MEM_DEV, TOK, BANK)
        hidden_hits, feature_hits = one_hots(member_seeds)
        mixing = jnp.einsum("mkb,mkc->mbc", feature_hits, hidden_hits)
        low_term = (NOISE_SCALE * jnp.einsum("mtb,mbc->mtc", projected, mixing)).astype(jnp.bfloat16)
        extra = lax.dot_general(low_term.reshape(MEM_DEV * TOK, BANK), bank_out, (((1,), (1,)), ((), ())), preferred_element_type=jnp.float32)
        return (base_part + extra).astype(jnp.bfloat16).reshape(MEM_DEV, TOK, FF)

    hidden = lax.map(forward, (grouped_tokens, grouped_seeds)).reshape(MEMBERS, TOK, FF)
    return hidden, new_weight
```

```python
import functools

import jax
import jax.numpy as jnp
from jax import lax
from jax.experimental import pallas as pl
from jax.experimental.pallas import tpu as pltpu
from jax.sharding import Mesh
from jax.sharding import PartitionSpec as P

POP = ("pop_0", "pop_1", "pop_2")
MESH = pl.DeviceIdType.MESH

NOISE_SCALE = 0.1
STEP_SCALE = 0.03

RING = 4
DEPTH = 8
FAR = 1 << 20
F32 = jnp.float32
BF16 = jnp.bfloat16


def nt(a, b):
    return lax.dot_general(a, b, (((1,), (1,)), ((), ())), preferred_element_type=F32)


def nn(a, b):
    return jnp.dot(a, b, preferred_element_type=F32)


def halves(a):
    high = a.astype(BF16)
    return high, (a - high.astype(F32)).astype(BF16)


def slot(da, db):
    return (da % RING) * RING + db % RING


def one_hot_row(levels, row):
    return levels == jnp.broadcast_to(row, levels.shape)


def kernel(
    tok_hbm, w_hbm, bi_hbm, bo_hbm, small_hbm, seeds_hbm, hidden_hbm, nw_hbm,
    tok, w, bi, bo, small, seeds, acc, out, nw, weights, coup, zz,
    send, recv, sib_send, sib_recv, z_send, z_recv, s_send, s_recv, tok_sem, local, done,
):
    x, y, c, z = (lax.axis_index(name) for name in (*POP, "row"))
    rows = w_hbm.shape[0]
    half = rows // 2
    mine = x, y
    other = 1 - c

    def place(da, db, color):
        px = (x + da * (1 - color) + db * color) % RING
        py = (y + da * color + db * (1 - color)) % RING
        return px, py

    def column_block(da, db, color):
        px, py = place(da, db, color)
        return (px * RING + py) * 2 + color

    def peer(da, db):
        px, py = place(da % RING, db % RING, c)
        return (px, py, c, z)

    ways = {"a+": (1, 0), "a-": (-1, 0), "b+": (0, 1), "b-": (0, -1)}
    sibling = (x, y, other, z)
    up, down = (x, y, c, (z + 1) % DEPTH), (x, y, c, (z + DEPTH - 1) % DEPTH)
    neighbours = [peer(*step) for step in ways.values()] + [sibling, up, down]

    barrier = pltpu.get_barrier_semaphore()
    for neighbour in neighbours:
        pl.semaphore_signal(barrier, inc=1, device_id=neighbour, device_id_type=MESH)
    pl.semaphore_wait(barrier, len(neighbours))

    pending = []

    def remote(src, dst, send_sem, recv_sem, target):
        return pltpu.make_async_remote_copy(
            src_ref=src, dst_ref=dst, send_sem=send_sem, recv_sem=recv_sem,
            device_id=target, device_id_type=MESH,
        )

    def go(copy):
        copy.start()
        pending.append(copy)

    def part(index, h):
        return w.at[index, pl.ds(h * half, half), :]

    order = {name: place_at for place_at, name in enumerate(ways)}

    def push(da, db, h, way):
        step = ways[way]
        there = slot(da - step[0], db - step[1])
        here = slot(da, db)
        source = w_hbm.at[pl.ds(h * half, half), :] if here == 0 else part(here, h)
        go(remote(source, part(there, h), send.at[order[way] * 32 + here * 2 + h],
                  recv.at[there * 2 + h], peer(*step)))

    def across(da, db, h):
        here = slot(da, db)
        source = w_hbm.at[pl.ds(h * half, half), :] if here == 0 else part(here, h)
        go(remote(source, part(16 + here, h), sib_send.at[here * 2 + h],
                  sib_recv.at[here * 2 + h], sibling))

    def arrive(da, db, h, *onward):
        here = slot(da, db)
        ref = part(here, h)
        remote(ref, ref, send.at[0], recv.at[here * 2 + h], sibling).wait_recv()
        for way in onward:
            push(da, db, h, way)
        across(da, db, h)

    def sib_arrive(da, db):
        here = slot(da, db)
        for h in range(2):
            ref = part(16 + here, h)
            remote(ref, ref, send.at[0], sib_recv.at[here * 2 + h], sibling).wait_recv()

    def small_push(source, target_ref, k, way):
        go(remote(source, target_ref, s_send.at[k], s_recv.at[k], peer(*ways[way])))

    def small_arrive(ref, k):
        remote(ref, ref, s_send.at[0], s_recv.at[k], sibling).wait_recv()

    small_push(small_hbm, small.at[0, 0, 3], 0, "a+")
    small_push(small_hbm, small.at[0, 0, 1], 1, "a-")
    for h, one, two in ((0, "a+", "b+"), (1, "a-", "b-")):
        push(0, 0, h, one)
        push(0, 0, h, two)

    own_w = [pltpu.make_async_copy(w_hbm, w.at[0], local.at[0])]
    own_w[0].start()
    across(0, 0, 0)
    across(0, 0, 1)

    def z_block(ref, first, count):
        return ref.at[pl.ds(first, count)]

    z_own = z_block(bi, z * 4, 4)
    go(remote(bi_hbm, z_own, z_send.at[0], z_recv.at[0], up))
    go(remote(bi_hbm, z_own, z_send.at[1], z_recv.at[4], down))
    own_bi = pltpu.make_async_copy(bi_hbm, z_own, local.at[1])
    own_bi.start()
    own_small = pltpu.make_async_copy(small_hbm, small.at[0, 0, 0], local.at[2])
    own_small.start()
    own_bo = pltpu.make_async_copy(bo_hbm, bo, local.at[3])
    own_bo.start()
    own_seeds = pltpu.make_async_copy(seeds_hbm, seeds, local.at[4])
    own_seeds.start()

    loads = {}
    for color, at in ((c, 0), (other, 16)):
        for da in range(RING):
            for db in range(RING):
                start = pl.multiple_of(column_block(da, db, color) * 128, 128)
                index = at + slot(da, db)
                loads[index] = pltpu.make_async_copy(
                    tok_hbm.at[:, pl.ds(start, 128)], tok.at[index], tok_sem.at[index]
                )
    sequence = [(0, 0), (-1, 0), (1, 0), (0, -1), (0, 1), (2, 0), (-1, -1), (-1, 1), (1, -1),
                (1, 1), (0, 2), (2, -1), (2, 1), (-1, 2), (1, 2), (2, 2)]
    for place_at in sequence:
        for at in (0, 16):
            loads[at + slot(*place_at)].start()

    def blocks_of(places):
        return [at + slot(*place_at) for place_at in places for at in (0, 16)]

    def multiply(places, mode):
        blocks = blocks_of(places)
        for place_at in places:
            sib_arrive(*place_at)
        for block in blocks:
            loads[block].wait()
        lhs = [tok[block] for block in blocks]
        extra = mode == "term"
        if extra:
            lhs += [zz[0], zz[1]]
        lhs = jnp.concatenate(lhs, axis=1)

        @pl.loop(0, 2)
        def _(h):
            span = pl.ds(pl.multiple_of(h * half, half), half)
            rhs = [w[block, span, :] for block in blocks]
            if extra:
                rhs += [bo[span, :], bo[span, :]]
            product = nt(lhs, jnp.concatenate(rhs, axis=1))
            if mode == "first":
                acc[h] = product
            elif mode == "last":
                out[h] = (acc[h] + product).astype(BF16)
                start = pl.multiple_of(h * half, half)
                pltpu.make_async_copy(
                    out.at[h], hidden_hbm.at[:, pl.ds(start, half)], done.at[h]
                ).start()
            else:
                acc[h] += product

    def z_arrive(k, behind, first, count):
        block = (z + DEPTH - behind) % DEPTH * 4 + first
        ref = z_block(bi, block, count)
        remote(ref, ref, z_send.at[0], z_recv.at[k], sibling).wait_recv()

    def z_relay(k, behind, first, count, target):
        block = (z + DEPTH - behind) % DEPTH * 4 + first
        ref = z_block(bi, block, count)
        go(remote(ref, ref, z_send.at[k], z_recv.at[k], target))

    small_arrive(small.at[0, 0, 3], 0)
    small_push(small.at[0, 0, 3], small.at[0, 0, 2], 2, "a+")
    small_arrive(small.at[0, 0, 1], 1)
    for h, one, two in ((1, "a+", "b+"), (0, "a-", "b-")):
        push(0, 0, h, one)
        push(0, 0, h, two)
    own_w[0].wait()
    own_small.wait()
    own_bi.wait()
    own_bo.wait()
    own_seeds.wait()

    z_arrive(0, 1, 0, 4)
    z_relay(2, 1, 0, 4, up)
    z_arrive(4, 7, 0, 4)
    z_relay(5, 7, 0, 4, down)

    arrive(-1, 0, 0, "a+", "b+", "b-")
    arrive(1, 0, 1, "a-", "b+", "b-")
    small_arrive(small.at[0, 0, 2], 2)
    small_push(small.at[0, 0], small.at[0, 3], 3, "b+")
    small_push(small.at[0, 0], small.at[0, 1], 4, "b-")
    arrive(0, -1, 0, "b+")
    arrive(0, 1, 1, "b-")

    z_arrive(2, 2, 0, 4)
    z_relay(3, 2, 0, 4, up)
    z_arrive(5, 6, 0, 4)
    z_relay(6, 6, 0, 4, down)

    arrive(-1, 0, 1, "b+", "b-")
    arrive(1, 0, 0, "b+", "b-")
    arrive(0, -1, 1)
    arrive(0, 1, 0)
    small_arrive(small.at[0, 3], 3)
    small_push(small.at[0, 3], small.at[0, 2], 5, "b+")
    small_arrive(small.at[0, 1], 4)
    multiply([(0, 0), (-1, 0)], "first")
    arrive(2, 0, 0, "b+", "b-")
    arrive(2, 0, 1, "b+", "b-")
    z_arrive(3, 3, 0, 4)
    z_half_up = z_block(bi, (z + DEPTH - 3) % DEPTH * 4, 2)
    go(remote(z_half_up, z_half_up, z_send.at[4], z_recv.at[1], up))
    z_arrive(6, 5, 0, 4)
    z_half_down = z_block(bi, (z + DEPTH - 5) % DEPTH * 4 + 2, 2)
    go(remote(z_half_down, z_half_down, z_send.at[7], z_recv.at[7], down))
    multiply([(1, 0), (0, -1)], "add")
    arrive(-1, -1, 0, "b+")
    arrive(-1, 1, 0)
    arrive(1, -1, 1)
    arrive(1, 1, 1, "b-")
    small_arrive(small.at[0, 2], 5)
    go(remote(small.at[0], small.at[1], s_send.at[6], s_recv.at[6], sibling))
    arrive(0, 2, 0)
    arrive(0, 2, 1)
    multiply([(0, 1), (2, 0)], "add")
    z_arrive(1, 4, 0, 2)
    z_arrive(7, 4, 2, 2)
    small_arrive(small.at[1], 6)

    lanes = lax.broadcasted_iota(jnp.int32, (16, 128), 1)
    fit = [small[color, :, :, 8, :].reshape(16, 128).astype(F32) for color in range(2)]
    packed = jnp.where(lanes < 64, fit[0], fit[1])
    columns = jnp.concatenate([packed, jnp.zeros((112, 128), F32)], axis=0).T
    sums = [jnp.zeros((8, 128), F32) for _ in range(16)]
    for j in range(16):
        column = jnp.broadcast_to(columns[:, j : j + 1], (128, 128))
        for m in range(16):
            sign = jnp.clip(packed[m : m + 1, :] - column, -1.0, 1.0)
            sums[m] += jnp.sum(sign.reshape(16, 8, 128), axis=0)
    ranks = jnp.concatenate([jnp.sum(s, axis=0, keepdims=True) for s in sums], axis=0) + 512.0
    turned = pltpu.roll(ranks, 64, 1)
    for color in range(2):
        low, high = (ranks, turned) if color == 0 else (turned, ranks)
        both = jnp.where(lanes < 64, low, high)
        coarse = jnp.floor(both * (1.0 / 16.0)) * 16.0
        weights[color, 0] = coarse
        weights[color, 1] = both - coarse

    arrive(-1, -1, 1)
    arrive(-1, 1, 1, "b-")
    arrive(1, -1, 0, "b+")
    arrive(1, 1, 0)

    levels = lax.broadcasted_iota(jnp.int32, (128, 128), 0)
    coup[...] = jnp.zeros_like(coup)

    def couple(color):
        @pl.loop(0, 16)
        def _(r):
            block = small[color, r // RING, r % RING]
            coarse = weights[color, 0, pl.ds(r, 1), :]
            fine = weights[color, 1, pl.ds(r, 1), :]
            hits, tops, rests = [], [], []
            for j in range(4):
                hits.append(one_hot_row(levels, block[j : j + 1]).astype(F32).astype(BF16))
                hit = one_hot_row(levels, block[4 + j : 5 + j])
                tops.append(jnp.where(hit, coarse, 0.0).astype(BF16))
                rests.append(jnp.where(hit, fine, 0.0).astype(BF16))
            rhs = jnp.concatenate(
                [jnp.concatenate(tops, axis=1), jnp.concatenate(rests, axis=1)], axis=0
            )
            coup[...] += nt(jnp.concatenate(hits, axis=1), rhs)

    couple(0)
    arrive(2, -1, 0, "b+")
    arrive(2, 1, 0)
    couple(1)
    arrive(2, -1, 1)
    arrive(2, 1, 1, "b-")
    multiply([(-1, -1), (-1, 1)], "add")

    coupling = (coup[:, :128] + coup[:, 128:]) * (STEP_SCALE / (2.0 * (16 * 96 - 1)))
    c_high, c_low = halves(coupling)
    own_in = bi[column_block(0, 0, c)]
    m_high, m_low = halves(nt(c_high, own_in) + nt(c_low, own_in))
    update = nn(jnp.concatenate([bo[...], bo[...]], axis=1), jnp.concatenate([m_high, m_low], axis=0))
    nw[...] = (w[0].astype(F32) + update).astype(BF16)
    nw_copy = pltpu.make_async_copy(nw, nw_hbm, done.at[2])
    nw_copy.start()
    multiply([(1, -1), (1, 1)], "add")
    arrive(-1, 2, 0)
    arrive(-1, 2, 1)

    def project(g, total):
        lhs, rhs = [], []
        for db in range(RING):
            color = (c + g // RING) % 2
            lhs.append(tok[g * RING + db])
            rhs.append(bi[column_block(g % RING, db, color)])
        return total + nn(jnp.concatenate(lhs, axis=1), jnp.concatenate(rhs, axis=0))

    for place_at in [(0, 2), (2, -1), (2, 1), (-1, 2), (1, 2), (2, 2)]:
        for at in (0, 16):
            loads[at + slot(*place_at)].wait()
            loads[at + slot(*place_at)] = None
    tokens = tok.shape[1]
    projected = lax.fori_loop(0, 2 * RING, project, jnp.zeros((tokens, 128), F32))
    p_high, p_low = halves(projected)
    outs, ins = [], []
    for j in range(4):
        outs.append(one_hot_row(levels, seeds[j : j + 1]).astype(F32).astype(BF16))
        ins.append(one_hot_row(levels, seeds[4 + j : 5 + j]).astype(F32).astype(BF16))
    ins = jnp.concatenate(ins, axis=1)
    picked = nn(jnp.concatenate([p_high, p_low], axis=1), jnp.concatenate([ins, ins], axis=0))
    member = lax.shift_right_logical(lax.broadcasted_iota(jnp.int32, picked.shape, 0), 4)
    lane = lax.broadcasted_iota(jnp.int32, picked.shape, 1) & 63
    g_high, g_low = halves(jnp.where(member == lane, picked * NOISE_SCALE, 0.0))
    term = nt(
        jnp.concatenate([p_high, p_low, p_high, g_high, g_low], axis=1),
        jnp.concatenate([c_high, c_high, c_low, *outs, *outs], axis=1),
    )
    z_high, z_low = halves(term)
    zz[0] = z_high
    zz[1] = z_low

    arrive(1, 2, 0)
    arrive(1, 2, 1)

    class Ready:
        def wait(self):
            pass

    for key in loads:
        loads[key] = loads[key] or Ready()
    multiply([(0, 2), (2, -1)], "term")
    arrive(2, 2, 0)
    arrive(2, 2, 1)
    multiply([(2, 1), (-1, 2)], "add")
    multiply([(1, 2), (2, 2)], "last")

    for copy in pending:
        copy.wait_send()
    nw_copy.wait()
    for h in range(2):
        pltpu.make_async_copy(out.at[h], hidden_hbm.at[:, pl.ds(h * half, half)], done.at[h]).wait()


def lane_packed(seeds):
    pairs = seeds.transpose(1, 2, 0).reshape(2, 4, 2, seeds.shape[0])
    pairs = jnp.pad(pairs, ((0, 0), (0, 0), (0, 0), (0, 64 - seeds.shape[0])), constant_values=-1)
    return pairs.reshape(8, 128)


def shards(tokens, weight, bank_in, bank_out, fitness, past_seeds, new_seeds):
    members, each, features = tokens.shape
    rows, wide = weight.shape
    flat = members * each
    levels = jnp.pad(
        jnp.broadcast_to(fitness, (2, members)), ((0, 0), (0, 64 - members)), constant_values=FAR
    ).reshape(1, 128)
    small = jnp.concatenate(
        [lane_packed(past_seeds), jnp.broadcast_to(levels, (8, 128))], axis=0
    )
    dma = pltpu.SemaphoreType.DMA
    hidden, new_weight = pl.pallas_call(
        kernel,
        out_shape=(
            jax.ShapeDtypeStruct((flat, rows), BF16),
            jax.ShapeDtypeStruct((rows, wide), BF16),
        ),
        in_specs=[pl.BlockSpec(memory_space=pl.ANY)] * 6,
        out_specs=[pl.BlockSpec(memory_space=pl.ANY)] * 2,
        scratch_shapes=[
            pltpu.VMEM((32, flat, 128), BF16),
            pltpu.VMEM((32, rows, 128), BF16),
            pltpu.VMEM((32, 128, 128), BF16),
            pltpu.VMEM((rows, 128), BF16),
            pltpu.VMEM((2, RING, RING, 16, 128), jnp.int32),
            pltpu.VMEM((8, 128), jnp.int32),
            pltpu.VMEM((2, flat, rows // 2), F32),
            pltpu.VMEM((2, flat, rows // 2), BF16),
            pltpu.VMEM((rows, 128), BF16),
            pltpu.VMEM((2, 2, 16, 128), F32),
            pltpu.VMEM((128, 256), F32),
            pltpu.VMEM((2, flat, 128), BF16),
            dma((128,)), dma((32,)), dma((32,)), dma((32,)), dma((8,)), dma((8,)),
            dma((7,)), dma((7,)), dma((32,)), dma((5,)), dma((3,)),
        ],
        compiler_params=pltpu.CompilerParams(
            collective_id=0, has_side_effects=True, vmem_limit_bytes=60 * 1024 * 1024
        ),
    )(
        tokens.reshape(flat, features), weight, bank_in.reshape(4, 128, 128), bank_out,
        small, lane_packed(new_seeds),
    )
    return hidden.reshape(members, each, rows), new_weight


def solution(mesh):
    torus = Mesh(
        mesh.devices.reshape(4, 4, 2, mesh.shape["row"]), ("pop_0", "pop_1", "pop_2", "row")
    )
    return jax.shard_map(
        shards,
        mesh=torus,
        in_specs=(
            P(POP, None, None),
            P("row", POP),
            P("row", None),
            P("row", None),
            P(POP),
            P(POP, None, None),
            P(POP, None, None),
        ),
        out_specs=(P(POP, None, "row"), P("row", POP)),
        check_vma=False,
    )
```

```python
import functools

import jax
import jax.numpy as jnp
from jax import lax
from jax.experimental import pallas as pl
from jax.experimental.pallas import tpu as pltpu
from jax.sharding import Mesh
from jax.sharding import PartitionSpec as P

POP = ("pop_0", "pop_1", "pop_2")
MESH = pl.DeviceIdType.MESH

NOISE_SCALE = 0.1
STEP_SCALE = 0.03

RING = 4
DEPTH = 8
FAR = 1 << 20
F32 = jnp.float32
BF16 = jnp.bfloat16


def nt(a, b):
    return lax.dot_general(a, b, (((1,), (1,)), ((), ())), preferred_element_type=F32)


def nn(a, b):
    return jnp.dot(a, b, preferred_element_type=F32)


def halves(a):
    high = a.astype(BF16)
    return high, (a - high.astype(F32)).astype(BF16)


def slot(da, db):
    return (da % RING) * RING + db % RING


def one_hot_row(levels, row):
    return levels == jnp.broadcast_to(row, levels.shape)


def kernel(
    tok_hbm, w_hbm, bi_hbm, bo_hbm, fit_hbm, past_hbm, seeds_hbm, out, nw,
    tok, w, bi, bo, past, fit, seeds, acc, weights, coup, shares, zz,
    send, recv, sib_send, sib_recv, z_send, z_recv, s_send, s_recv, tok_sem, local,
):
    x, y, c, z = (lax.axis_index(name) for name in (*POP, "row"))
    rows = w_hbm.shape[0]
    half = rows // 2
    other = 1 - c

    def place(da, db, color):
        px = (x + da * (1 - color) + db * color) % RING
        py = (y + da * color + db * (1 - color)) % RING
        return px, py

    def column_block(da, db, color):
        px, py = place(da, db, color)
        return (px * RING + py) * 2 + color

    def peer(da, db):
        px, py = place(da % RING, db % RING, c)
        return (px, py, c, z)

    ways = {"a+": (1, 0), "a-": (-1, 0), "b+": (0, 1), "b-": (0, -1)}
    sibling = (x, y, other, z)
    up, down = (x, y, c, (z + 1) % DEPTH), (x, y, c, (z + DEPTH - 1) % DEPTH)
    neighbours = [peer(*step) for step in ways.values()] + [sibling, up, down]

    barrier = pltpu.get_barrier_semaphore()
    for neighbour in neighbours:
        pl.semaphore_signal(barrier, inc=1, device_id=neighbour, device_id_type=MESH)
    pl.semaphore_wait(barrier, len(neighbours))

    pending = []

    def remote(src, dst, send_sem, recv_sem, target):
        return pltpu.make_async_remote_copy(
            src_ref=src, dst_ref=dst, send_sem=send_sem, recv_sem=recv_sem,
            device_id=target, device_id_type=MESH,
        )

    def go(copy):
        copy.start()
        pending.append(copy)

    def part(index, h):
        return w.at[index, pl.ds(h * half, half), :]

    order = {name: place_at for place_at, name in enumerate(ways)}

    def push(da, db, h, way):
        step = ways[way]
        there = slot(da - step[0], db - step[1])
        here = slot(da, db)
        source = w_hbm.at[pl.ds(h * half, half), :] if here == 0 else part(here, h)
        go(remote(source, part(there, h), send.at[order[way] * 32 + here * 2 + h],
                  recv.at[there * 2 + h], peer(*step)))

    def across(da, db, h):
        here = slot(da, db)
        source = w_hbm.at[pl.ds(h * half, half), :] if here == 0 else part(here, h)
        go(remote(source, part(16 + here, h), sib_send.at[here * 2 + h],
                  sib_recv.at[here * 2 + h], sibling))

    def arrive(da, db, h, *onward):
        here = slot(da, db)
        ref = part(here, h)
        remote(ref, ref, send.at[0], recv.at[here * 2 + h], sibling).wait_recv()
        for way in onward:
            push(da, db, h, way)
        across(da, db, h)

    def sib_arrive(da, db):
        here = slot(da, db)
        for h in range(2):
            ref = part(16 + here, h)
            remote(ref, ref, send.at[0], sib_recv.at[here * 2 + h], sibling).wait_recv()

    def small_push(k, way, first, there, count):
        for j, (ref, own) in enumerate(((past, past_hbm), (fit, fit_hbm))):
            if count == 1:
                source = own if first == 0 else ref.at[0, first]
                target = ref.at[0, there]
            else:
                source = ref.at[0, pl.ds(first, count)]
                target = ref.at[0, pl.ds(there, count)]
            go(remote(source, target, s_send.at[2 * k + j], s_recv.at[2 * k + j],
                      peer(*ways[way])))

    def small_arrive(k, there, count):
        for j, ref in enumerate((past, fit)):
            ref = ref.at[0, there] if count == 1 else ref.at[0, pl.ds(there, count)]
            remote(ref, ref, s_send.at[0], s_recv.at[2 * k + j], sibling).wait_recv()

    small_push(0, "a+", 0, 3, 1)
    small_push(1, "a-", 0, 1, 1)
    for h, one, two in ((0, "a+", "b+"), (1, "a-", "b-")):
        push(0, 0, h, one)
        push(0, 0, h, two)

    own_w = [pltpu.make_async_copy(w_hbm, w.at[0], local.at[0])]
    own_w[0].start()
    across(0, 0, 0)
    across(0, 0, 1)

    def z_block(ref, first, count):
        return ref.at[pl.ds(first, count)]

    z_own = z_block(bi, z * 4, 4)
    go(remote(bi_hbm, z_own, z_send.at[0], z_recv.at[0], up))
    go(remote(bi_hbm, z_own, z_send.at[1], z_recv.at[4], down))
    own_bi = pltpu.make_async_copy(bi_hbm, z_own, local.at[1])
    own_bi.start()
    own_past = pltpu.make_async_copy(past_hbm, past.at[0, 0], local.at[2])
    own_past.start()
    own_fit = pltpu.make_async_copy(fit_hbm, fit.at[0, 0], local.at[5])
    own_fit.start()
    own_bo = pltpu.make_async_copy(bo_hbm, bo, local.at[3])
    own_bo.start()
    own_seeds = pltpu.make_async_copy(seeds_hbm, seeds, local.at[4])
    own_seeds.start()

    loads = {}
    for color, at in ((c, 0), (other, 16)):
        for da in range(RING):
            for db in range(RING):
                start = pl.multiple_of(column_block(da, db, color) * 128, 128)
                index = at + slot(da, db)
                loads[index] = pltpu.make_async_copy(
                    tok_hbm.at[:, pl.ds(start, 128)], tok.at[index], tok_sem.at[index]
                )
    sequence = [(0, 0), (-1, 0), (1, 0), (0, -1), (0, 1), (2, 0), (0, 2), (-1, -1), (-1, 1),
                (1, -1), (1, 1), (2, -1), (2, 1), (-1, 2), (1, 2), (2, 2)]
    for place_at in sequence:
        for at in (0, 16):
            loads[at + slot(*place_at)].start()

    def blocks_of(places):
        return [at + slot(*place_at) for place_at in places for at in (0, 16)]

    def multiply(places, mode):
        blocks = blocks_of(places)
        for place_at in places:
            sib_arrive(*place_at)
        for block in blocks:
            if block in loads:
                loads.pop(block).wait()
        lhs = [tok[block] for block in blocks]
        extra = mode == "term"
        if extra:
            lhs += [zz[0], zz[1]]
        lhs = jnp.concatenate(lhs, axis=1)

        @pl.loop(0, 2)
        def _(h):
            span = pl.ds(pl.multiple_of(h * half, half), half)
            rhs = [w[block, span, :] for block in blocks]
            if extra:
                rhs += [bo[span, :], bo[span, :]]
            product = nt(lhs, jnp.concatenate(rhs, axis=1))
            if mode == "first":
                acc[h] = product
            elif mode == "last":
                out[:, span] = (acc[h] + product).astype(BF16)
            else:
                acc[h] += product

    def z_arrive(k, behind, first, count):
        block = (z + DEPTH - behind) % DEPTH * 4 + first
        ref = z_block(bi, block, count)
        remote(ref, ref, z_send.at[0], z_recv.at[k], sibling).wait_recv()

    def z_relay(k, behind, first, count, target):
        block = (z + DEPTH - behind) % DEPTH * 4 + first
        ref = z_block(bi, block, count)
        go(remote(ref, ref, z_send.at[k], z_recv.at[k], target))

    lanes = lax.broadcasted_iota(jnp.int32, (8, 128), 1)

    def padded(rows, filler):
        return jnp.concatenate(
            [rows, jnp.full((rows.shape[0], 128 - rows.shape[1]), filler, rows.dtype)], axis=1
        )

    def paired(rows):
        rows = padded(rows, -1)
        return jnp.where(lanes < 64, rows, pltpu.roll(pltpu.roll(rows, 4, 0), 64, 1))

    small_arrive(0, 3, 1)
    small_push(2, "a+", 3, 2, 1)
    small_arrive(1, 1, 1)
    for h, one, two in ((1, "a+", "b+"), (0, "a-", "b-")):
        push(0, 0, h, one)
        push(0, 0, h, two)
    own_w[0].wait()
    own_past.wait()
    own_fit.wait()
    own_bi.wait()
    own_bo.wait()
    own_seeds.wait()
    multiply([(0, 0)], "first")

    small_arrive(2, 2, 1)
    small_push(3, "b+", 0, 12, 4)
    small_push(4, "b-", 0, 4, 4)
    z_arrive(0, 1, 0, 4)
    z_relay(2, 1, 0, 4, up)
    z_arrive(4, 7, 0, 4)
    z_relay(5, 7, 0, 4, down)

    arrive(-1, 0, 0, "a+", "b+", "b-")
    arrive(1, 0, 1, "a-", "b+", "b-")
    arrive(0, -1, 0, "b+")
    arrive(0, 1, 1, "b-")

    z_arrive(2, 2, 0, 4)
    z_relay(3, 2, 0, 4, up)
    z_arrive(5, 6, 0, 4)
    z_relay(6, 6, 0, 4, down)
    small_arrive(3, 12, 4)
    small_push(5, "b+", 12, 8, 4)
    small_arrive(4, 4, 4)

    arrive(-1, 0, 1, "b+", "b-")
    arrive(1, 0, 0, "b+", "b-")
    arrive(0, -1, 1)
    arrive(0, 1, 0)
    z_arrive(3, 3, 0, 4)
    z_half_up = z_block(bi, (z + DEPTH - 3) % DEPTH * 4, 2)
    go(remote(z_half_up, z_half_up, z_send.at[4], z_recv.at[1], up))
    z_arrive(6, 5, 0, 4)
    z_half_down = z_block(bi, (z + DEPTH - 5) % DEPTH * 4 + 2, 2)
    go(remote(z_half_down, z_half_down, z_send.at[7], z_recv.at[7], down))
    multiply([(-1, 0), (1, 0)], "add")
    small_arrive(5, 8, 4)
    go(remote(fit.at[0], fit.at[1], s_send.at[12], s_recv.at[12], sibling))
    multiply([(0, -1), (0, 1)], "add")
    arrive(2, 0, 0, "b+", "b-")
    arrive(2, 0, 1, "b+", "b-")
    arrive(-1, -1, 0, "b+")
    arrive(-1, 1, 0)

    remote(fit.at[0], fit.at[1], s_send.at[12], s_recv.at[12], sibling).wait_recv()
    wide = lax.broadcasted_iota(jnp.int32, (16, 128), 1)
    mine, theirs = (
        padded(jnp.concatenate([fit[k, r] for r in range(16)], axis=0), FAR).astype(F32)
        for k in range(2)
    )
    everyone = jnp.where(wide < 64, mine, pltpu.roll(theirs, 64, 1))
    columns = jnp.concatenate([everyone, jnp.zeros((112, 128), F32)], axis=0).T
    packed = jnp.where(lanes < 64, mine[:8], pltpu.roll(mine[8:], 64, 1))
    sums = [jnp.zeros((8, 128), F32) for _ in range(8)]
    for j in range(16):
        column = jnp.broadcast_to(columns[:, j : j + 1], (128, 128))
        for m in range(8):
            sign = jnp.clip(packed[m : m + 1, :] - column, -1.0, 1.0)
            sums[m] += jnp.sum(sign.reshape(16, 8, 128), axis=0)
    ranks = jnp.concatenate([jnp.sum(s, axis=0, keepdims=True) for s in sums], axis=0) + 512.0
    turned = pltpu.roll(ranks, 64, 1)
    for first, low, high in ((0, ranks, turned), (8, turned, ranks)):
        both = jnp.where(lanes < 64, low, high)
        coarse = jnp.floor(both * (1.0 / 16.0)) * 16.0
        weights[0, first : first + 8] = coarse
        weights[1, first : first + 8] = both - coarse

    arrive(1, -1, 1)
    arrive(1, 1, 1, "b-")

    levels = lax.broadcasted_iota(jnp.int32, (128, 128), 0)

    def hot(rows):
        return [one_hot_row(levels, rows[j : j + 1]).astype(F32).astype(BF16) for j in range(4)]

    coup[...] = jnp.zeros_like(coup)

    def couple(first, last):
        @pl.loop(first, last)
        def _(r):
            coarse = weights[0, pl.ds(r, 1), :]
            fine = weights[1, pl.ds(r, 1), :]
            features = paired(past[0, r, 1])
            tops, rests = [], []
            for j in range(4):
                hit = one_hot_row(levels, features[j : j + 1])
                tops.append(jnp.where(hit, coarse, 0.0).astype(BF16))
                rests.append(jnp.where(hit, fine, 0.0).astype(BF16))
            lhs = jnp.concatenate(
                [jnp.concatenate(tops, axis=1), jnp.concatenate(rests, axis=1)], axis=0
            )
            coup[...] += nt(lhs, jnp.concatenate(hot(paired(past[0, r, 0])), axis=1))

    couple(0, 8)
    arrive(0, 2, 0)
    arrive(0, 2, 1)
    couple(8, 16)
    shares[0] = coup[:128, :] + coup[128:, :]
    arrive(-1, -1, 1)
    arrive(-1, 1, 1, "b-")
    multiply([(2, 0), (0, 2)], "add")
    go(remote(shares.at[0], shares.at[1], s_send.at[13], s_recv.at[13], sibling))
    arrive(1, -1, 0, "b+")
    arrive(1, 1, 0)
    multiply([(-1, -1), (-1, 1)], "add")
    z_arrive(1, 4, 0, 2)
    z_arrive(7, 4, 2, 2)

    for block in sorted(loads):
        loads.pop(block).wait()
    def project(g, total):
        lhs, rhs = [], []
        for db in range(RING):
            color = (c + g // RING) % 2
            lhs.append(tok[g * RING + db])
            rhs.append(bi[column_block(g % RING, db, color)])
        return total + nn(jnp.concatenate(lhs, axis=1), jnp.concatenate(rhs, axis=0))

    tokens = tok.shape[1]
    projected = lax.fori_loop(0, 2 * RING, project, jnp.zeros((tokens, 128), F32))
    p_high, p_low = halves(projected)
    arrive(2, -1, 0, "b+")
    arrive(2, 1, 0)
    multiply([(1, -1), (1, 1)], "add")

    remote(shares.at[0], shares.at[1], s_send.at[13], s_recv.at[13], sibling).wait_recv()
    coupling = ((shares[0] + shares[1]) * (STEP_SCALE / (2.0 * (16 * 96 - 1)))).T
    c_high, c_low = halves(coupling)
    own_in = bi[column_block(0, 0, c)]
    m_high, m_low = halves(nt(c_high, own_in) + nt(c_low, own_in))
    update = nn(jnp.concatenate([bo[...], bo[...]], axis=1), jnp.concatenate([m_high, m_low], axis=0))
    nw[...] = (w[0].astype(F32) + update).astype(BF16)
    arrive(2, -1, 1)
    arrive(2, 1, 1, "b-")

    outs, ins = hot(paired(seeds[0])), jnp.concatenate(hot(paired(seeds[1])), axis=1)
    picked = nn(jnp.concatenate([p_high, p_low], axis=1), jnp.concatenate([ins, ins], axis=0))
    member = lax.shift_right_logical(lax.broadcasted_iota(jnp.int32, picked.shape, 0), 4)
    lane = lax.broadcasted_iota(jnp.int32, picked.shape, 1) & 63
    g_high, g_low = halves(jnp.where(member == lane, picked * NOISE_SCALE, 0.0))
    term = nt(
        jnp.concatenate([p_high, p_low, p_high, g_high, g_low], axis=1),
        jnp.concatenate([c_high, c_high, c_low, *outs, *outs], axis=1),
    )
    z_high, z_low = halves(term)
    zz[0] = z_high
    zz[1] = z_low
    multiply([(2, -1), (2, 1)], "term")
    arrive(-1, 2, 0)
    arrive(-1, 2, 1)
    arrive(1, 2, 0)
    arrive(1, 2, 1)
    multiply([(-1, 2), (1, 2)], "add")
    arrive(2, 2, 0)
    arrive(2, 2, 1)
    multiply([(2, 2)], "last")

    for copy in pending:
        copy.wait_send()


def shards(tokens, weight, bank_in, bank_out, fitness, past_seeds, new_seeds):
    members, each, features = tokens.shape
    rows, wide = weight.shape
    flat = members * each
    seeds = (*past_seeds.shape[1:], members)
    dma = pltpu.SemaphoreType.DMA
    hidden, new_weight = pl.pallas_call(
        kernel,
        out_shape=(
            pltpu.VMEM((flat, rows), BF16),
            pltpu.VMEM((rows, wide), BF16),
        ),
        in_specs=[pl.BlockSpec(memory_space=pl.ANY)] * 7,
        out_specs=[pl.BlockSpec(memory_space=pltpu.VMEM)] * 2,
        scratch_shapes=[
            pltpu.VMEM((32, flat, 128), BF16),
            pltpu.VMEM((32, rows, 128), BF16),
            pltpu.VMEM((32, 128, 128), BF16),
            pltpu.VMEM((rows, 128), BF16),
            pltpu.VMEM((2, 16, *seeds), jnp.int32),
            pltpu.VMEM((2, 16, 1, members), jnp.int32),
            pltpu.VMEM(seeds, jnp.int32),
            pltpu.VMEM((2, flat, rows // 2), F32),
            pltpu.VMEM((2, 16, 128), F32),
            pltpu.VMEM((256, 128), F32),
            pltpu.VMEM((2, 128, 128), F32),
            pltpu.VMEM((2, flat, 128), BF16),
            dma((128,)), dma((32,)), dma((32,)), dma((32,)), dma((8,)), dma((8,)),
            dma((14,)), dma((14,)), dma((32,)), dma((6,)),
        ],
        compiler_params=pltpu.CompilerParams(
            collective_id=0, has_side_effects=True, vmem_limit_bytes=56 * 1024 * 1024
        ),
    )(
        tokens.reshape(flat, features), weight, bank_in.reshape(4, 128, 128), bank_out,
        fitness.reshape(1, members), past_seeds.transpose(1, 2, 0), new_seeds.transpose(1, 2, 0),
    )
    return hidden.reshape(members, each, rows), new_weight


def solution(mesh):
    torus = Mesh(
        mesh.devices.reshape(4, 4, 2, mesh.shape["row"]), ("pop_0", "pop_1", "pop_2", "row")
    )
    return jax.shard_map(
        shards,
        mesh=torus,
        in_specs=(
            P(POP, None, None),
            P("row", POP),
            P("row", None),
            P("row", None),
            P(POP),
            P(POP, None, None),
            P(POP, None, None),
        ),
        out_specs=(P(POP, None, "row"), P("row", POP)),
        check_vma=False,
    )
```

```python
import functools

import jax
import jax.numpy as jnp
from jax import lax
from jax.experimental import pallas as pl
from jax.experimental.pallas import tpu as pltpu
from jax.sharding import Mesh
from jax.sharding import PartitionSpec as P

POP = ("pop_0", "pop_1", "pop_2")
MESH = pl.DeviceIdType.MESH

NOISE_SCALE = 0.1
STEP_SCALE = 0.03

RING = 4
DEPTH = 8
FAR = 1 << 20
F32 = jnp.float32
BF16 = jnp.bfloat16


def nt(a, b):
    return lax.dot_general(a, b, (((1,), (1,)), ((), ())), preferred_element_type=F32)


def nn(a, b):
    return jnp.dot(a, b, preferred_element_type=F32)


def halves(a):
    high = a.astype(BF16)
    return high, (a - high.astype(F32)).astype(BF16)


def slot(da, db):
    return (da % RING) * RING + db % RING


def one_hot_row(levels, row):
    return levels == jnp.broadcast_to(row, levels.shape)


def kernel(
    tok_hbm, w_hbm, bi_hbm, bo_hbm, fit_hbm, past_hbm, seeds_hbm, out, nw,
    tok, w, bi, bo, past, fit, seeds, acc, weights, coup, shares, zz,
    send, recv, sib_send, sib_recv, z_send, z_recv, s_send, s_recv, tok_sem, local,
):
    x, y, c, z = (lax.axis_index(name) for name in (*POP, "row"))
    rows = w_hbm.shape[0]
    half = rows // 2
    other = 1 - c

    def place(da, db, color):
        px = (x + da * (1 - color) + db * color) % RING
        py = (y + da * color + db * (1 - color)) % RING
        return px, py

    def column_block(da, db, color):
        px, py = place(da, db, color)
        return (px * RING + py) * 2 + color

    def peer(da, db):
        px, py = place(da % RING, db % RING, c)
        return (px, py, c, z)

    ways = {"a+": (1, 0), "a-": (-1, 0), "b+": (0, 1), "b-": (0, -1)}
    sibling = (x, y, other, z)
    up, down = (x, y, c, (z + 1) % DEPTH), (x, y, c, (z + DEPTH - 1) % DEPTH)
    neighbours = [peer(*step) for step in ways.values()] + [sibling, up, down]

    barrier = pltpu.get_barrier_semaphore()
    for neighbour in neighbours:
        pl.semaphore_signal(barrier, inc=1, device_id=neighbour, device_id_type=MESH)
    pl.semaphore_wait(barrier, len(neighbours))

    pending = []

    def remote(src, dst, send_sem, recv_sem, target):
        return pltpu.make_async_remote_copy(
            src_ref=src, dst_ref=dst, send_sem=send_sem, recv_sem=recv_sem,
            device_id=target, device_id_type=MESH,
        )

    def go(copy):
        copy.start()
        pending.append(copy)

    def part(index, h):
        return w.at[index, pl.ds(h * half, half), :]

    order = {name: place_at for place_at, name in enumerate(ways)}

    def push(da, db, h, way):
        step = ways[way]
        there = slot(da - step[0], db - step[1])
        here = slot(da, db)
        source = w_hbm.at[pl.ds(h * half, half), :] if here == 0 else part(here, h)
        go(remote(source, part(there, h), send.at[order[way] * 32 + here * 2 + h],
                  recv.at[there * 2 + h], peer(*step)))

    def across(da, db, h):
        here = slot(da, db)
        source = w_hbm.at[pl.ds(h * half, half), :] if here == 0 else part(here, h)
        go(remote(source, part(16 + here, h), sib_send.at[here * 2 + h],
                  sib_recv.at[here * 2 + h], sibling))

    def arrive(da, db, h, *onward):
        here = slot(da, db)
        ref = part(here, h)
        remote(ref, ref, send.at[0], recv.at[here * 2 + h], sibling).wait_recv()
        for way in onward:
            push(da, db, h, way)
        across(da, db, h)

    def sib_arrive(da, db):
        here = slot(da, db)
        for h in range(2):
            ref = part(16 + here, h)
            remote(ref, ref, send.at[0], sib_recv.at[here * 2 + h], sibling).wait_recv()

    def small_push(k, way, first, there, count):
        for j, (ref, own) in enumerate(((past, past_hbm), (fit, fit_hbm))):
            if count == 1:
                source = own if first == 0 else ref.at[0, first]
                target = ref.at[0, there]
            else:
                source = ref.at[0, pl.ds(first, count)]
                target = ref.at[0, pl.ds(there, count)]
            go(remote(source, target, s_send.at[2 * k + j], s_recv.at[2 * k + j],
                      peer(*ways[way])))

    def small_arrive(k, there, count):
        for j, ref in enumerate((past, fit)):
            ref = ref.at[0, there] if count == 1 else ref.at[0, pl.ds(there, count)]
            remote(ref, ref, s_send.at[0], s_recv.at[2 * k + j], sibling).wait_recv()

    small_push(0, "a+", 0, 3, 1)
    small_push(1, "a-", 0, 1, 1)
    push(0, 0, 0, "a+")
    push(0, 0, 1, "a-")

    own_w = [pltpu.make_async_copy(w_hbm, w.at[0], local.at[0])]
    own_w[0].start()
    across(0, 0, 0)
    across(0, 0, 1)

    def z_block(ref, first, count):
        return ref.at[pl.ds(first, count)]

    z_own = z_block(bi, z * 4, 4)
    go(remote(bi_hbm, z_own, z_send.at[0], z_recv.at[0], up))
    go(remote(bi_hbm, z_own, z_send.at[1], z_recv.at[4], down))
    own_bi = pltpu.make_async_copy(bi_hbm, z_own, local.at[1])
    own_bi.start()
    own_past = pltpu.make_async_copy(past_hbm, past.at[0, 0], local.at[2])
    own_past.start()
    own_fit = pltpu.make_async_copy(fit_hbm, fit.at[0, 0], local.at[5])
    own_fit.start()
    own_bo = pltpu.make_async_copy(bo_hbm, bo, local.at[3])
    own_bo.start()
    own_seeds = pltpu.make_async_copy(seeds_hbm, seeds, local.at[4])
    own_seeds.start()

    loads = {}
    for color, at in ((c, 0), (other, 16)):
        for da in range(RING):
            for db in range(RING):
                start = pl.multiple_of(column_block(da, db, color) * 128, 128)
                index = at + slot(da, db)
                loads[index] = pltpu.make_async_copy(
                    tok_hbm.at[:, pl.ds(start, 128)], tok.at[index], tok_sem.at[index]
                )
    sequence = [(0, 0), (-1, 0), (1, 0), (0, -1), (0, 1), (2, 0), (0, 2), (-1, -1), (-1, 1),
                (1, -1), (1, 1), (2, -1), (2, 1), (-1, 2), (1, 2), (2, 2)]
    for place_at in sequence:
        for at in (0, 16):
            loads[at + slot(*place_at)].start()

    def blocks_of(places):
        return [at + slot(*place_at) for place_at in places for at in (0, 16)]

    def multiply(places, mode):
        blocks = blocks_of(places)
        for place_at in places:
            sib_arrive(*place_at)
        for block in blocks:
            if block in loads:
                loads.pop(block).wait()
        lhs = [tok[block] for block in blocks]
        extra = mode == "term"
        if extra:
            lhs += [zz[0], zz[1]]
        lhs = jnp.concatenate(lhs, axis=1)

        @pl.loop(0, 2)
        def _(h):
            span = pl.ds(pl.multiple_of(h * half, half), half)
            rhs = [w[block, span, :] for block in blocks]
            if extra:
                rhs += [bo[span, :], bo[span, :]]
            product = nt(lhs, jnp.concatenate(rhs, axis=1))
            if mode == "first":
                acc[h] = product
            elif mode == "last":
                out[:, span] = (acc[h] + product).astype(BF16)
            else:
                acc[h] += product

    def z_arrive(k, behind, first, count):
        block = (z + DEPTH - behind) % DEPTH * 4 + first
        ref = z_block(bi, block, count)
        remote(ref, ref, z_send.at[0], z_recv.at[k], sibling).wait_recv()

    def z_relay(k, behind, first, count, target):
        block = (z + DEPTH - behind) % DEPTH * 4 + first
        ref = z_block(bi, block, count)
        go(remote(ref, ref, z_send.at[k], z_recv.at[k], target))

    lanes = lax.broadcasted_iota(jnp.int32, (8, 128), 1)

    def padded(rows, filler):
        return jnp.concatenate(
            [rows, jnp.full((rows.shape[0], 128 - rows.shape[1]), filler, rows.dtype)], axis=1
        )

    def paired(rows):
        rows = padded(rows, -1)
        return jnp.where(lanes < 64, rows, pltpu.roll(pltpu.roll(rows, 4, 0), 64, 1))

    small_arrive(0, 3, 1)
    small_push(2, "a+", 3, 2, 1)
    small_arrive(1, 1, 1)
    push(0, 0, 1, "a+")
    push(0, 0, 0, "a-")
    own_past.wait()
    own_fit.wait()
    small_arrive(2, 2, 1)
    small_push(3, "b+", 0, 12, 4)
    small_push(4, "b-", 0, 4, 4)
    push(0, 0, 0, "b+")
    push(0, 0, 1, "b-")
    arrive(-1, 0, 0, "a+")
    arrive(1, 0, 1, "a-")
    own_w[0].wait()
    own_bi.wait()
    own_bo.wait()
    own_seeds.wait()
    multiply([(0, 0)], "first")
    small_arrive(3, 12, 4)
    small_push(5, "b+", 12, 8, 4)
    small_arrive(4, 4, 4)
    push(0, 0, 1, "b+")
    push(0, 0, 0, "b-")
    for da, h in ((-1, 0), (1, 1)):
        push(da, 0, h, "b+")
        push(da, 0, h, "b-")
    z_arrive(0, 1, 0, 4)
    z_relay(2, 1, 0, 4, up)
    z_arrive(4, 7, 0, 4)
    z_relay(5, 7, 0, 4, down)
    arrive(-1, 0, 1, "b+", "b-")
    arrive(1, 0, 0, "b+", "b-")
    arrive(0, -1, 0, "b+")
    arrive(0, 1, 1, "b-")
    z_arrive(2, 2, 0, 4)
    z_relay(3, 2, 0, 4, up)
    z_arrive(5, 6, 0, 4)
    z_relay(6, 6, 0, 4, down)
    small_arrive(5, 8, 4)
    go(remote(fit.at[0], fit.at[1], s_send.at[12], s_recv.at[12], sibling))
    multiply([(-1, 0), (1, 0)], "add")
    arrive(2, 0, 0, "b+", "b-")
    arrive(2, 0, 1, "b+", "b-")

    remote(fit.at[0], fit.at[1], s_send.at[12], s_recv.at[12], sibling).wait_recv()
    wide = lax.broadcasted_iota(jnp.int32, (16, 128), 1)
    mine, theirs = (
        padded(jnp.concatenate([fit[k, r] for r in range(16)], axis=0), FAR).astype(F32)
        for k in range(2)
    )
    everyone = jnp.where(wide < 64, mine, pltpu.roll(theirs, 64, 1))
    columns = jnp.concatenate([everyone, jnp.zeros((112, 128), F32)], axis=0).T
    packed = jnp.where(lanes < 64, mine[:8], pltpu.roll(mine[8:], 64, 1))
    sums = [jnp.zeros((8, 128), F32) for _ in range(8)]
    for j in range(16):
        column = jnp.broadcast_to(columns[:, j : j + 1], (128, 128))
        for m in range(8):
            sign = jnp.clip(packed[m : m + 1, :] - column, -1.0, 1.0)
            sums[m] += jnp.sum(sign.reshape(16, 8, 128), axis=0)
    ranks = jnp.concatenate([jnp.sum(s, axis=0, keepdims=True) for s in sums], axis=0) + 512.0
    turned = pltpu.roll(ranks, 64, 1)
    for first, low, high in ((0, ranks, turned), (8, turned, ranks)):
        both = jnp.where(lanes < 64, low, high)
        coarse = jnp.floor(both * (1.0 / 16.0)) * 16.0
        weights[0, first : first + 8] = coarse
        weights[1, first : first + 8] = both - coarse

    arrive(0, -1, 1)
    arrive(0, 1, 0)

    levels = lax.broadcasted_iota(jnp.int32, (128, 128), 0)

    def hot(rows):
        return [one_hot_row(levels, rows[j : j + 1]).astype(F32).astype(BF16) for j in range(4)]

    coup[...] = jnp.zeros_like(coup)

    def couple(first, last):
        @pl.loop(first, last)
        def _(r):
            coarse = weights[0, pl.ds(r, 1), :]
            fine = weights[1, pl.ds(r, 1), :]
            features = paired(past[0, r, 1])
            tops, rests = [], []
            for j in range(4):
                hit = one_hot_row(levels, features[j : j + 1])
                tops.append(jnp.where(hit, coarse, 0.0).astype(BF16))
                rests.append(jnp.where(hit, fine, 0.0).astype(BF16))
            lhs = jnp.concatenate(
                [jnp.concatenate(tops, axis=1), jnp.concatenate(rests, axis=1)], axis=0
            )
            coup[...] += nt(lhs, jnp.concatenate(hot(paired(past[0, r, 0])), axis=1))

    couple(0, 8)
    arrive(-1, -1, 0, "b+")
    arrive(-1, 1, 0)
    z_arrive(3, 3, 0, 4)
    z_half_up = z_block(bi, (z + DEPTH - 3) % DEPTH * 4, 2)
    go(remote(z_half_up, z_half_up, z_send.at[4], z_recv.at[1], up))
    z_arrive(6, 5, 0, 4)
    z_half_down = z_block(bi, (z + DEPTH - 5) % DEPTH * 4 + 2, 2)
    go(remote(z_half_down, z_half_down, z_send.at[7], z_recv.at[7], down))
    couple(8, 16)
    shares[0] = coup[:128, :] + coup[128:, :]
    multiply([(0, -1), (0, 1)], "add")
    go(remote(shares.at[0], shares.at[1], s_send.at[13], s_recv.at[13], sibling))
    arrive(1, -1, 1)
    arrive(1, 1, 1, "b-")
    z_arrive(1, 4, 0, 2)
    z_arrive(7, 4, 2, 2)

    for block in sorted(loads):
        loads.pop(block).wait()
    def project(g, total):
        lhs, rhs = [], []
        for db in range(RING):
            color = (c + g // RING) % 2
            lhs.append(tok[g * RING + db])
            rhs.append(bi[column_block(g % RING, db, color)])
        return total + nn(jnp.concatenate(lhs, axis=1), jnp.concatenate(rhs, axis=0))

    tokens = tok.shape[1]
    projected = lax.fori_loop(0, 2 * RING, project, jnp.zeros((tokens, 128), F32))
    p_high, p_low = halves(projected)
    arrive(-1, -1, 1)
    arrive(-1, 1, 1, "b-")
    remote(shares.at[0], shares.at[1], s_send.at[13], s_recv.at[13], sibling).wait_recv()
    coupling = ((shares[0] + shares[1]) * (STEP_SCALE / (2.0 * (16 * 96 - 1)))).T
    c_high, c_low = halves(coupling)
    own_in = bi[column_block(0, 0, c)]
    m_high, m_low = halves(nt(c_high, own_in) + nt(c_low, own_in))
    update = nn(jnp.concatenate([bo[...], bo[...]], axis=1), jnp.concatenate([m_high, m_low], axis=0))
    nw[...] = (w[0].astype(F32) + update).astype(BF16)
    arrive(1, -1, 0, "b+")
    arrive(1, 1, 0)
    multiply([(-1, -1), (-1, 1)], "add")
    arrive(0, 2, 0)
    arrive(0, 2, 1)
    multiply([(1, -1), (1, 1)], "add")
    outs, ins = hot(paired(seeds[0])), jnp.concatenate(hot(paired(seeds[1])), axis=1)
    picked = nn(jnp.concatenate([p_high, p_low], axis=1), jnp.concatenate([ins, ins], axis=0))
    member = lax.shift_right_logical(lax.broadcasted_iota(jnp.int32, picked.shape, 0), 4)
    lane = lax.broadcasted_iota(jnp.int32, picked.shape, 1) & 63
    g_high, g_low = halves(jnp.where(member == lane, picked * NOISE_SCALE, 0.0))
    term = nt(
        jnp.concatenate([p_high, p_low, p_high, g_high, g_low], axis=1),
        jnp.concatenate([c_high, c_high, c_low, *outs, *outs], axis=1),
    )
    z_high, z_low = halves(term)
    zz[0] = z_high
    zz[1] = z_low
    arrive(2, -1, 0, "b+")
    arrive(2, 1, 0)
    multiply([(2, 0), (0, 2)], "term")
    arrive(2, -1, 1)
    arrive(2, 1, 1, "b-")
    multiply([(2, -1), (2, 1)], "add")
    arrive(-1, 2, 0)
    arrive(-1, 2, 1)
    arrive(1, 2, 0)
    arrive(1, 2, 1)
    multiply([(-1, 2), (1, 2)], "add")
    arrive(2, 2, 0)
    arrive(2, 2, 1)
    multiply([(2, 2)], "last")

    for copy in pending:
        copy.wait_send()


def finish(out, nw, hidden_hbm, nw_hbm, done):
    third = out.shape[0] // 3
    copies = [pltpu.make_async_copy(nw, nw_hbm, done.at[3])]
    for k in range(3):
        span = pl.ds(k * third, third)
        copies.append(pltpu.make_async_copy(out.at[span], hidden_hbm.at[span], done.at[k]))
    for copy in copies:
        copy.start()
    for copy in copies:
        copy.wait()


def shards(tokens, weight, bank_in, bank_out, fitness, past_seeds, new_seeds):
    members, each, features = tokens.shape
    rows, wide = weight.shape
    flat = members * each
    seeds = (*past_seeds.shape[1:], members)
    dma = pltpu.SemaphoreType.DMA
    hidden, new_weight = pl.pallas_call(
        kernel,
        out_shape=(
            pltpu.VMEM((flat, rows), BF16),
            pltpu.VMEM((rows, wide), BF16),
        ),
        in_specs=[pl.BlockSpec(memory_space=pl.ANY)] * 7,
        out_specs=[pl.BlockSpec(memory_space=pltpu.VMEM)] * 2,
        scratch_shapes=[
            pltpu.VMEM((32, flat, 128), BF16),
            pltpu.VMEM((32, rows, 128), BF16),
            pltpu.VMEM((32, 128, 128), BF16),
            pltpu.VMEM((rows, 128), BF16),
            pltpu.VMEM((2, 16, *seeds), jnp.int32),
            pltpu.VMEM((2, 16, 1, members), jnp.int32),
            pltpu.VMEM(seeds, jnp.int32),
            pltpu.VMEM((2, flat, rows // 2), F32),
            pltpu.VMEM((2, 16, 128), F32),
            pltpu.VMEM((256, 128), F32),
            pltpu.VMEM((2, 128, 128), F32),
            pltpu.VMEM((2, flat, 128), BF16),
            dma((128,)), dma((32,)), dma((32,)), dma((32,)), dma((8,)), dma((8,)),
            dma((14,)), dma((14,)), dma((32,)), dma((6,)),
        ],
        compiler_params=pltpu.CompilerParams(
            collective_id=0, has_side_effects=True, vmem_limit_bytes=56 * 1024 * 1024
        ),
    )(
        tokens.reshape(flat, features), weight, bank_in.reshape(4, 128, 128), bank_out,
        fitness.reshape(1, members), past_seeds.transpose(1, 2, 0), new_seeds.transpose(1, 2, 0),
    )
    hidden, new_weight = pl.pallas_call(
        finish,
        out_shape=(
            jax.ShapeDtypeStruct((flat, rows), BF16),
            jax.ShapeDtypeStruct((rows, wide), BF16),
        ),
        in_specs=[pl.BlockSpec(memory_space=pltpu.VMEM)] * 2,
        out_specs=[pl.BlockSpec(memory_space=pl.ANY)] * 2,
        scratch_shapes=[dma((4,))],
        compiler_params=pltpu.CompilerParams(vmem_limit_bytes=32 * 1024 * 1024),
    )(hidden, new_weight)
    return hidden.reshape(members, each, rows), new_weight


def solution(mesh):
    torus = Mesh(
        mesh.devices.reshape(4, 4, 2, mesh.shape["row"]), ("pop_0", "pop_1", "pop_2", "row")
    )
    return jax.shard_map(
        shards,
        mesh=torus,
        in_specs=(
            P(POP, None, None),
            P("row", POP),
            P("row", None),
            P("row", None),
            P(POP),
            P(POP, None, None),
            P(POP, None, None),
        ),
        out_specs=(P(POP, None, "row"), P("row", POP)),
        check_vma=False,
    )
```

```python
import functools

import jax
import jax.numpy as jnp
from jax import lax
from jax.experimental import pallas as pl
from jax.experimental.pallas import tpu as pltpu
from jax.sharding import Mesh
from jax.sharding import PartitionSpec as P

POP = ("pop_0", "pop_1", "pop_2")
MESH = pl.DeviceIdType.MESH

NOISE_SCALE = 0.1
STEP_SCALE = 0.03

RING = 4
DEPTH = 8
FAR = 1 << 20
F32 = jnp.float32
BF16 = jnp.bfloat16


def nt(a, b):
    return lax.dot_general(a, b, (((1,), (1,)), ((), ())), preferred_element_type=F32)


def nn(a, b):
    return jnp.dot(a, b, preferred_element_type=F32)


def halves(a):
    high = a.astype(BF16)
    return high, (a - high.astype(F32)).astype(BF16)


def slot(da, db):
    return (da % RING) * RING + db % RING


LAST = (slot(2, 2), 16 + slot(2, 2))


def one_hot_row(levels, row):
    return levels == jnp.broadcast_to(row, levels.shape)


def kernel(
    tok_hbm, w_hbm, bi_hbm, bo_hbm, fit_hbm, past_hbm, seeds_hbm,
    acc, w_last, tok_last, nw,
    tok, w, bi, bo, past, fit, seeds, weights, coup, shares, zz,
    send, recv, sib_send, sib_recv, z_send, z_recv, s_send, s_recv, tok_sem, local,
):
    x, y, c, z = (lax.axis_index(name) for name in (*POP, "row"))
    rows = w_hbm.shape[0]
    half = rows // 2
    other = 1 - c

    def place(da, db, color):
        px = (x + da * (1 - color) + db * color) % RING
        py = (y + da * color + db * (1 - color)) % RING
        return px, py

    def column_block(da, db, color):
        px, py = place(da, db, color)
        return (px * RING + py) * 2 + color

    def peer(da, db):
        px, py = place(da % RING, db % RING, c)
        return (px, py, c, z)

    ways = {"a+": (1, 0), "a-": (-1, 0), "b+": (0, 1), "b-": (0, -1)}
    sibling = (x, y, other, z)
    up, down = (x, y, c, (z + 1) % DEPTH), (x, y, c, (z + DEPTH - 1) % DEPTH)
    neighbours = [peer(*step) for step in ways.values()] + [sibling, up, down]

    barrier = pltpu.get_barrier_semaphore()
    for neighbour in neighbours:
        pl.semaphore_signal(barrier, inc=1, device_id=neighbour, device_id_type=MESH)
    pl.semaphore_wait(barrier, len(neighbours))

    pending = []

    def remote(src, dst, send_sem, recv_sem, target):
        return pltpu.make_async_remote_copy(
            src_ref=src, dst_ref=dst, send_sem=send_sem, recv_sem=recv_sem,
            device_id=target, device_id_type=MESH,
        )

    def go(copy):
        copy.start()
        pending.append(copy)

    def part(index, h):
        block = w_last.at[index // 16] if index in LAST else w.at[index]
        return block.at[pl.ds(h * half, half), :]

    order = {name: place_at for place_at, name in enumerate(ways)}

    def push(da, db, h, way):
        step = ways[way]
        there = slot(da - step[0], db - step[1])
        here = slot(da, db)
        source = w_hbm.at[pl.ds(h * half, half), :] if here == 0 else part(here, h)
        go(remote(source, part(there, h), send.at[order[way] * 32 + here * 2 + h],
                  recv.at[there * 2 + h], peer(*step)))

    def across(da, db, h):
        here = slot(da, db)
        source = w_hbm.at[pl.ds(h * half, half), :] if here == 0 else part(here, h)
        go(remote(source, part(16 + here, h), sib_send.at[here * 2 + h],
                  sib_recv.at[here * 2 + h], sibling))

    def arrive(da, db, h, *onward):
        here = slot(da, db)
        ref = part(here, h)
        remote(ref, ref, send.at[0], recv.at[here * 2 + h], sibling).wait_recv()
        for way in onward:
            push(da, db, h, way)
        across(da, db, h)

    def sib_arrive(da, db):
        here = slot(da, db)
        for h in range(2):
            ref = part(16 + here, h)
            remote(ref, ref, send.at[0], sib_recv.at[here * 2 + h], sibling).wait_recv()

    def small_push(k, way, first, there, count):
        for j, (ref, own) in enumerate(((past, past_hbm), (fit, fit_hbm))):
            if count == 1:
                source = own if first == 0 else ref.at[0, first]
                target = ref.at[0, there]
            else:
                source = ref.at[0, pl.ds(first, count)]
                target = ref.at[0, pl.ds(there, count)]
            go(remote(source, target, s_send.at[2 * k + j], s_recv.at[2 * k + j],
                      peer(*ways[way])))

    def small_arrive(k, there, count):
        for j, ref in enumerate((past, fit)):
            ref = ref.at[0, there] if count == 1 else ref.at[0, pl.ds(there, count)]
            remote(ref, ref, s_send.at[0], s_recv.at[2 * k + j], sibling).wait_recv()

    small_push(0, "a+", 0, 3, 1)
    small_push(1, "a-", 0, 1, 1)
    push(0, 0, 0, "a+")
    push(0, 0, 1, "a-")

    own_w = [pltpu.make_async_copy(w_hbm, w.at[0], local.at[0])]
    own_w[0].start()
    across(0, 0, 0)
    across(0, 0, 1)

    def z_block(ref, first, count):
        return ref.at[pl.ds(first, count)]

    z_own = z_block(bi, z * 4, 4)
    go(remote(bi_hbm, z_own, z_send.at[0], z_recv.at[0], up))
    go(remote(bi_hbm, z_own, z_send.at[1], z_recv.at[4], down))
    own_bi = pltpu.make_async_copy(bi_hbm, z_own, local.at[1])
    own_bi.start()
    own_past = pltpu.make_async_copy(past_hbm, past.at[0, 0], local.at[2])
    own_past.start()
    own_fit = pltpu.make_async_copy(fit_hbm, fit.at[0, 0], local.at[5])
    own_fit.start()
    own_bo = pltpu.make_async_copy(bo_hbm, bo, local.at[3])
    own_bo.start()
    own_seeds = pltpu.make_async_copy(seeds_hbm, seeds, local.at[4])
    own_seeds.start()

    loads = {}
    for color, at in ((c, 0), (other, 16)):
        for da in range(RING):
            for db in range(RING):
                start = pl.multiple_of(column_block(da, db, color) * 128, 128)
                index = at + slot(da, db)
                loads[index] = pltpu.make_async_copy(
                    tok_hbm.at[:, pl.ds(start, 128)], tok.at[index], tok_sem.at[index]
                )
                if index in LAST:
                    loads[32 + index // 16] = pltpu.make_async_copy(
                        tok_hbm.at[:, pl.ds(start, 128)],
                        tok_last.at[index // 16],
                        tok_sem.at[32 + index // 16],
                    )
    sequence = [(0, 0), (-1, 0), (1, 0), (0, -1), (0, 1), (2, 0), (0, 2), (-1, -1), (-1, 1),
                (1, -1), (1, 1), (2, -1), (2, 1), (-1, 2), (1, 2), (2, 2)]
    for place_at in sequence:
        for at in (0, 16):
            loads[at + slot(*place_at)].start()
    loads[32].start()
    loads[33].start()

    def blocks_of(places):
        return [at + slot(*place_at) for place_at in places for at in (0, 16)]

    def multiply(places, mode):
        blocks = blocks_of(places)
        for place_at in places:
            sib_arrive(*place_at)
        for block in blocks:
            if block in loads:
                loads.pop(block).wait()
        lhs = [tok[block] for block in blocks]
        extra = mode == "term"
        if extra:
            lhs += [zz[0], zz[1]]
        lhs = jnp.concatenate(lhs, axis=1)

        rhs = [w[block] for block in blocks]
        if extra:
            rhs += [bo[...], bo[...]]
        product = nt(lhs, jnp.concatenate(rhs, axis=1))
        if mode == "first":
            acc[...] = product
        else:
            acc[...] += product

    def z_arrive(k, behind, first, count):
        block = (z + DEPTH - behind) % DEPTH * 4 + first
        ref = z_block(bi, block, count)
        remote(ref, ref, z_send.at[0], z_recv.at[k], sibling).wait_recv()

    def z_relay(k, behind, first, count, target):
        block = (z + DEPTH - behind) % DEPTH * 4 + first
        ref = z_block(bi, block, count)
        go(remote(ref, ref, z_send.at[k], z_recv.at[k], target))

    lanes = lax.broadcasted_iota(jnp.int32, (8, 128), 1)

    def padded(rows, filler):
        return jnp.concatenate(
            [rows, jnp.full((rows.shape[0], 128 - rows.shape[1]), filler, rows.dtype)], axis=1
        )

    def paired(rows):
        rows = padded(rows, -1)
        return jnp.where(lanes < 64, rows, pltpu.roll(pltpu.roll(rows, 4, 0), 64, 1))

    small_arrive(0, 3, 1)
    small_push(2, "a+", 3, 2, 1)
    small_arrive(1, 1, 1)
    push(0, 0, 1, "a+")
    push(0, 0, 0, "a-")
    own_past.wait()
    own_fit.wait()
    small_arrive(2, 2, 1)
    small_push(3, "b+", 0, 12, 4)
    small_push(4, "b-", 0, 4, 4)
    push(0, 0, 0, "b+")
    push(0, 0, 1, "b-")
    arrive(-1, 0, 0, "a+")
    arrive(1, 0, 1, "a-")
    own_w[0].wait()
    own_bi.wait()
    own_bo.wait()
    own_seeds.wait()
    multiply([(0, 0)], "first")
    small_arrive(3, 12, 4)
    small_push(5, "b+", 12, 8, 4)
    small_arrive(4, 4, 4)
    push(0, 0, 1, "b+")
    push(0, 0, 0, "b-")
    for da, h in ((-1, 0), (1, 1)):
        push(da, 0, h, "b+")
        push(da, 0, h, "b-")
    z_arrive(0, 1, 0, 4)
    z_relay(2, 1, 0, 4, up)
    z_arrive(4, 7, 0, 4)
    z_relay(5, 7, 0, 4, down)
    arrive(-1, 0, 1, "b+", "b-")
    arrive(1, 0, 0, "b+", "b-")
    arrive(0, -1, 0, "b+")
    arrive(0, 1, 1, "b-")
    z_arrive(2, 2, 0, 4)
    z_relay(3, 2, 0, 4, up)
    z_arrive(5, 6, 0, 4)
    z_relay(6, 6, 0, 4, down)
    small_arrive(5, 8, 4)
    go(remote(fit.at[0], fit.at[1], s_send.at[12], s_recv.at[12], sibling))
    multiply([(-1, 0), (1, 0)], "add")
    arrive(2, 0, 0, "b+", "b-")
    arrive(2, 0, 1, "b+", "b-")

    remote(fit.at[0], fit.at[1], s_send.at[12], s_recv.at[12], sibling).wait_recv()
    wide = lax.broadcasted_iota(jnp.int32, (16, 128), 1)
    mine, theirs = (
        padded(jnp.concatenate([fit[k, r] for r in range(16)], axis=0), FAR).astype(F32)
        for k in range(2)
    )
    everyone = jnp.where(wide < 64, mine, pltpu.roll(theirs, 64, 1))
    columns = jnp.concatenate([everyone, jnp.zeros((112, 128), F32)], axis=0).T
    packed = jnp.where(lanes < 64, mine[:8], pltpu.roll(mine[8:], 64, 1))
    sums = [jnp.zeros((8, 128), F32) for _ in range(8)]
    for j in range(16):
        column = jnp.broadcast_to(columns[:, j : j + 1], (128, 128))
        for m in range(8):
            sign = jnp.clip(packed[m : m + 1, :] - column, -1.0, 1.0)
            sums[m] += jnp.sum(sign.reshape(16, 8, 128), axis=0)
    ranks = jnp.concatenate([jnp.sum(s, axis=0, keepdims=True) for s in sums], axis=0) + 512.0
    turned = pltpu.roll(ranks, 64, 1)
    for first, low, high in ((0, ranks, turned), (8, turned, ranks)):
        both = jnp.where(lanes < 64, low, high)
        coarse = jnp.floor(both * (1.0 / 16.0)) * 16.0
        weights[0, first : first + 8] = coarse
        weights[1, first : first + 8] = both - coarse

    arrive(0, -1, 1)
    arrive(0, 1, 0)

    levels = lax.broadcasted_iota(jnp.int32, (128, 128), 0)

    def hot(rows):
        return [one_hot_row(levels, rows[j : j + 1]).astype(F32).astype(BF16) for j in range(4)]

    coup[...] = jnp.zeros_like(coup)

    def couple(first, last):
        @pl.loop(first, last)
        def _(r):
            coarse = weights[0, pl.ds(r, 1), :]
            fine = weights[1, pl.ds(r, 1), :]
            features = paired(past[0, r, 1])
            tops, rests = [], []
            for j in range(4):
                hit = one_hot_row(levels, features[j : j + 1])
                tops.append(jnp.where(hit, coarse, 0.0).astype(BF16))
                rests.append(jnp.where(hit, fine, 0.0).astype(BF16))
            lhs = jnp.concatenate(
                [jnp.concatenate(tops, axis=1), jnp.concatenate(rests, axis=1)], axis=0
            )
            coup[...] += nt(lhs, jnp.concatenate(hot(paired(past[0, r, 0])), axis=1))

    couple(0, 8)
    arrive(-1, -1, 0, "b+")
    arrive(-1, 1, 0)
    z_arrive(3, 3, 0, 4)
    z_half_up = z_block(bi, (z + DEPTH - 3) % DEPTH * 4, 2)
    go(remote(z_half_up, z_half_up, z_send.at[4], z_recv.at[1], up))
    z_arrive(6, 5, 0, 4)
    z_half_down = z_block(bi, (z + DEPTH - 5) % DEPTH * 4 + 2, 2)
    go(remote(z_half_down, z_half_down, z_send.at[7], z_recv.at[7], down))
    couple(8, 16)
    shares[0] = coup[:128, :] + coup[128:, :]
    multiply([(0, -1), (0, 1)], "add")
    go(remote(shares.at[0], shares.at[1], s_send.at[13], s_recv.at[13], sibling))
    arrive(1, -1, 1)
    arrive(1, 1, 1, "b-")
    z_arrive(1, 4, 0, 2)
    z_arrive(7, 4, 2, 2)

    for block in sorted(loads):
        loads.pop(block).wait()
    def project(g, total):
        lhs, rhs = [], []
        for db in range(RING):
            color = (c + g // RING) % 2
            lhs.append(tok[g * RING + db])
            rhs.append(bi[column_block(g % RING, db, color)])
        return total + nn(jnp.concatenate(lhs, axis=1), jnp.concatenate(rhs, axis=0))

    tokens = tok.shape[1]
    projected = lax.fori_loop(0, 2 * RING, project, jnp.zeros((tokens, 128), F32))
    p_high = projected.astype(BF16)
    arrive(-1, -1, 1)
    arrive(-1, 1, 1, "b-")
    remote(shares.at[0], shares.at[1], s_send.at[13], s_recv.at[13], sibling).wait_recv()
    coupling = ((shares[0] + shares[1]) * (STEP_SCALE / (2.0 * (16 * 96 - 1)))).T
    c_high, c_low = halves(coupling)
    own_in = bi[column_block(0, 0, c)]
    m_high, m_low = halves(nt(c_high, own_in) + nt(c_low, own_in))
    update = nn(jnp.concatenate([bo[...], bo[...]], axis=1), jnp.concatenate([m_high, m_low], axis=0))
    nw[...] = (w[0].astype(F32) + update).astype(BF16)
    arrive(1, -1, 0, "b+")
    arrive(1, 1, 0)
    multiply([(-1, -1), (-1, 1)], "add")
    arrive(0, 2, 0)
    arrive(0, 2, 1)
    multiply([(1, -1), (1, 1)], "add")
    outs, ins = hot(paired(seeds[0])), jnp.concatenate(hot(paired(seeds[1])), axis=1)
    picked = nn(p_high, ins)
    member = lax.shift_right_logical(lax.broadcasted_iota(jnp.int32, picked.shape, 0), 4)
    lane = lax.broadcasted_iota(jnp.int32, picked.shape, 1) & 63
    own_picks = jnp.where(member == lane, picked, 0.0).astype(BF16)
    term = NOISE_SCALE * nt(own_picks, jnp.concatenate(outs, axis=1)) + nt(
        jnp.concatenate([p_high, p_high], axis=1), jnp.concatenate([c_high, c_low], axis=1)
    )
    z_high, z_low = halves(term)
    zz[0] = z_high
    zz[1] = z_low
    arrive(2, -1, 0, "b+")
    arrive(2, 1, 0)
    multiply([(2, 0), (0, 2)], "term")
    arrive(2, -1, 1)
    arrive(2, 1, 1, "b-")
    multiply([(2, -1), (2, 1)], "add")
    arrive(-1, 2, 0)
    arrive(-1, 2, 1)
    arrive(1, 2, 0)
    arrive(1, 2, 1)
    multiply([(-1, 2), (1, 2)], "add")
    arrive(2, 2, 0)
    arrive(2, 2, 1)
    sib_arrive(2, 2)

    for copy in pending:
        copy.wait_send()


def finish(acc, w_last, tok_last, nw, hidden_hbm, nw_hbm, out, done):
    weights_out = pltpu.make_async_copy(nw, nw_hbm, done.at[2])
    weights_out.start()
    lhs = jnp.concatenate([tok_last[0], tok_last[1]], axis=1)
    first = out.shape[1] * 4 // 7
    copies = []
    for k, (start, size) in enumerate(((0, first), (first, out.shape[1] - first))):
        span = pl.ds(start, size)
        rhs = jnp.concatenate([w_last[0, span, :], w_last[1, span, :]], axis=1)
        out[:, span] = (acc[:, span] + nt(lhs, rhs)).astype(BF16)
        copies.append(pltpu.make_async_copy(out.at[:, span], hidden_hbm.at[:, span], done.at[k]))
        copies[-1].start()
    for copy in copies:
        copy.wait()
    weights_out.wait()


def shards(tokens, weight, bank_in, bank_out, fitness, past_seeds, new_seeds):
    members, each, features = tokens.shape
    rows, wide = weight.shape
    flat = members * each
    seeds = (*past_seeds.shape[1:], members)
    dma = pltpu.SemaphoreType.DMA
    parts = pl.pallas_call(
        kernel,
        out_shape=(
            pltpu.VMEM((flat, rows), F32),
            pltpu.VMEM((2, rows, 128), BF16),
            pltpu.VMEM((2, flat, 128), BF16),
            pltpu.VMEM((rows, wide), BF16),
        ),
        in_specs=[pl.BlockSpec(memory_space=pl.ANY)] * 7,
        out_specs=[pl.BlockSpec(memory_space=pltpu.VMEM)] * 4,
        scratch_shapes=[
            pltpu.VMEM((32, flat, 128), BF16),
            pltpu.VMEM((32, rows, 128), BF16),
            pltpu.VMEM((32, 128, 128), BF16),
            pltpu.VMEM((rows, 128), BF16),
            pltpu.VMEM((2, 16, *seeds), jnp.int32),
            pltpu.VMEM((2, 16, 1, members), jnp.int32),
            pltpu.VMEM(seeds, jnp.int32),
            pltpu.VMEM((2, 16, 128), F32),
            pltpu.VMEM((256, 128), F32),
            pltpu.VMEM((2, 128, 128), F32),
            pltpu.VMEM((2, flat, 128), BF16),
            dma((128,)), dma((32,)), dma((32,)), dma((32,)), dma((8,)), dma((8,)),
            dma((14,)), dma((14,)), dma((34,)), dma((6,)),
        ],
        compiler_params=pltpu.CompilerParams(
            collective_id=0, has_side_effects=True, vmem_limit_bytes=52 * 1024 * 1024
        ),
    )(
        tokens.reshape(flat, features), weight, bank_in.reshape(4, 128, 128), bank_out,
        fitness.reshape(1, members), past_seeds.transpose(1, 2, 0), new_seeds.transpose(1, 2, 0),
    )
    hidden, new_weight = pl.pallas_call(
        finish,
        out_shape=(
            jax.ShapeDtypeStruct((flat, rows), BF16),
            jax.ShapeDtypeStruct((rows, wide), BF16),
        ),
        in_specs=[pl.BlockSpec(memory_space=pltpu.VMEM)] * 4,
        out_specs=[pl.BlockSpec(memory_space=pl.ANY)] * 2,
        scratch_shapes=[pltpu.VMEM((flat, rows), BF16), dma((3,))],
        compiler_params=pltpu.CompilerParams(vmem_limit_bytes=32 * 1024 * 1024),
    )(*parts)
    return hidden.reshape(members, each, rows), new_weight


def solution(mesh):
    torus = Mesh(
        mesh.devices.reshape(4, 4, 2, mesh.shape["row"]), ("pop_0", "pop_1", "pop_2", "row")
    )
    return jax.shard_map(
        shards,
        mesh=torus,
        in_specs=(
            P(POP, None, None),
            P("row", POP),
            P("row", None),
            P("row", None),
            P(POP),
            P(POP, None, None),
            P(POP, None, None),
        ),
        out_specs=(P(POP, None, "row"), P("row", POP)),
        check_vma=False,
    )
```

```python
import functools

import jax
import jax.numpy as jnp
from jax import lax
from jax.experimental import pallas as pl
from jax.experimental.pallas import tpu as pltpu
from jax.sharding import Mesh
from jax.sharding import PartitionSpec as P

POP = ("pop_0", "pop_1", "pop_2")
MESH = pl.DeviceIdType.MESH

NOISE_SCALE = 0.1
STEP_SCALE = 0.03

RING = 4
DEPTH = 8
FAR = 1 << 20
F32 = jnp.float32
BF16 = jnp.bfloat16


def nt(a, b):
    return lax.dot_general(a, b, (((1,), (1,)), ((), ())), preferred_element_type=F32)


def nn(a, b):
    return jnp.dot(a, b, preferred_element_type=F32)


def halves(a):
    high = a.astype(BF16)
    return high, (a - high.astype(F32)).astype(BF16)


def slot(da, db):
    return (da % RING) * RING + db % RING


LAST = (slot(2, 2), 16 + slot(2, 2))


def one_hot_row(levels, row):
    return levels == jnp.broadcast_to(row, levels.shape)


def kernel(
    tok_hbm, w_hbm, bi_hbm, bo_hbm, fit_hbm, past_hbm, seeds_hbm,
    acc, w_last, tok_last, nw,
    tok, w, bi, bo, past, fit, seeds, weights, coup, shares, zz,
    send, recv, sib_send, sib_recv, z_send, z_recv, s_send, s_recv, tok_sem, local,
):
    x, y, c, z = (lax.axis_index(name) for name in (*POP, "row"))
    rows = w_hbm.shape[0]
    half = rows // 2
    other = 1 - c

    def place(da, db, color):
        px = (x + da * (1 - color) + db * color) % RING
        py = (y + da * color + db * (1 - color)) % RING
        return px, py

    def column_block(da, db, color):
        px, py = place(da, db, color)
        return (px * RING + py) * 2 + color

    def peer(da, db):
        px, py = place(da % RING, db % RING, c)
        return (px, py, c, z)

    ways = {"a+": (1, 0), "a-": (-1, 0), "b+": (0, 1), "b-": (0, -1)}
    sibling = (x, y, other, z)
    up, down = (x, y, c, (z + 1) % DEPTH), (x, y, c, (z + DEPTH - 1) % DEPTH)
    neighbours = [peer(*step) for step in ways.values()] + [sibling, up, down]

    barrier = pltpu.get_barrier_semaphore()
    for neighbour in neighbours:
        pl.semaphore_signal(barrier, inc=1, device_id=neighbour, device_id_type=MESH)
    pl.semaphore_wait(barrier, len(neighbours))

    pending = []

    def remote(src, dst, send_sem, recv_sem, target):
        return pltpu.make_async_remote_copy(
            src_ref=src, dst_ref=dst, send_sem=send_sem, recv_sem=recv_sem,
            device_id=target, device_id_type=MESH,
        )

    def go(copy):
        copy.start()
        pending.append(copy)

    def part(index, h):
        block = w_last.at[index // 16] if index in LAST else w.at[index]
        return block.at[pl.ds(h * half, half), :]

    order = {name: place_at for place_at, name in enumerate(ways)}

    def push(da, db, h, way):
        step = ways[way]
        there = slot(da - step[0], db - step[1])
        here = slot(da, db)
        source = w_hbm.at[pl.ds(h * half, half), :] if here == 0 else part(here, h)
        go(remote(source, part(there, h), send.at[order[way] * 32 + here * 2 + h],
                  recv.at[there * 2 + h], peer(*step)))

    def across(da, db, h):
        here = slot(da, db)
        source = w_hbm.at[pl.ds(h * half, half), :] if here == 0 else part(here, h)
        go(remote(source, part(16 + here, h), sib_send.at[here * 2 + h],
                  sib_recv.at[here * 2 + h], sibling))

    def arrive(da, db, h, *onward):
        here = slot(da, db)
        ref = part(here, h)
        remote(ref, ref, send.at[0], recv.at[here * 2 + h], sibling).wait_recv()
        for way in onward:
            push(da, db, h, way)
        across(da, db, h)

    def sib_arrive(da, db):
        here = slot(da, db)
        for h in range(2):
            ref = part(16 + here, h)
            remote(ref, ref, send.at[0], sib_recv.at[here * 2 + h], sibling).wait_recv()

    def small_push(k, way, first, there, count):
        for j, (ref, own) in enumerate(((past, past_hbm), (fit, fit_hbm))):
            if count == 1:
                source = own if first == 0 else ref.at[0, first]
                target = ref.at[0, there]
            else:
                source = ref.at[0, pl.ds(first, count)]
                target = ref.at[0, pl.ds(there, count)]
            go(remote(source, target, s_send.at[2 * k + j], s_recv.at[2 * k + j],
                      peer(*ways[way])))

    def small_arrive(k, there, count):
        for j, ref in enumerate((past, fit)):
            ref = ref.at[0, there] if count == 1 else ref.at[0, pl.ds(there, count)]
            remote(ref, ref, s_send.at[0], s_recv.at[2 * k + j], sibling).wait_recv()

    small_push(0, "a+", 0, 3, 1)
    small_push(1, "a-", 0, 1, 1)
    push(0, 0, 0, "a+")
    push(0, 0, 1, "a-")

    own_w = [pltpu.make_async_copy(w_hbm, w.at[0], local.at[0])]
    own_w[0].start()
    across(0, 0, 0)
    across(0, 0, 1)

    def z_block(ref, first, count):
        return ref.at[pl.ds(first, count)]

    z_own = z_block(bi, z * 4, 4)
    go(remote(bi_hbm, z_own, z_send.at[0], z_recv.at[0], up))
    go(remote(bi_hbm, z_own, z_send.at[1], z_recv.at[4], down))
    own_bi = pltpu.make_async_copy(bi_hbm, z_own, local.at[1])
    own_bi.start()
    own_past = pltpu.make_async_copy(past_hbm, past.at[0, 0], local.at[2])
    own_past.start()
    own_fit = pltpu.make_async_copy(fit_hbm, fit.at[0, 0], local.at[5])
    own_fit.start()
    own_bo = pltpu.make_async_copy(bo_hbm, bo, local.at[3])
    own_bo.start()
    own_seeds = pltpu.make_async_copy(seeds_hbm, seeds, local.at[4])
    own_seeds.start()

    loads = {}
    for color, at in ((c, 0), (other, 16)):
        for da in range(RING):
            for db in range(RING):
                start = pl.multiple_of(column_block(da, db, color) * 128, 128)
                index = at + slot(da, db)
                loads[index] = pltpu.make_async_copy(
                    tok_hbm.at[:, pl.ds(start, 128)], tok.at[index], tok_sem.at[index]
                )
                if index in LAST:
                    loads[32 + index // 16] = pltpu.make_async_copy(
                        tok_hbm.at[:, pl.ds(start, 128)],
                        tok_last.at[index // 16],
                        tok_sem.at[32 + index // 16],
                    )
    sequence = [(0, 0), (-1, 0), (1, 0), (0, -1), (0, 1), (2, 0), (0, 2), (-1, -1), (-1, 1),
                (1, -1), (1, 1), (2, -1), (2, 1), (-1, 2), (1, 2), (2, 2)]
    for place_at in sequence:
        for at in (0, 16):
            loads[at + slot(*place_at)].start()
    loads[32].start()
    loads[33].start()

    def blocks_of(places):
        return [at + slot(*place_at) for place_at in places for at in (0, 16)]

    def multiply(places, mode):
        blocks = blocks_of(places)
        for place_at in places:
            sib_arrive(*place_at)
        for block in blocks:
            if block in loads:
                loads.pop(block).wait()
        lhs = [tok[block] for block in blocks]
        extra = mode == "term"
        if extra:
            lhs += [zz[0], zz[1]]
        lhs = jnp.concatenate(lhs, axis=1)

        rhs = [w[block] for block in blocks]
        if extra:
            rhs += [bo[...], bo[...]]
        product = nt(lhs, jnp.concatenate(rhs, axis=1))
        if mode == "first":
            acc[...] = product
        else:
            acc[...] += product

    def z_arrive(k, behind, first, count):
        block = (z + DEPTH - behind) % DEPTH * 4 + first
        ref = z_block(bi, block, count)
        remote(ref, ref, z_send.at[0], z_recv.at[k], sibling).wait_recv()

    def z_relay(k, behind, first, count, target):
        block = (z + DEPTH - behind) % DEPTH * 4 + first
        ref = z_block(bi, block, count)
        go(remote(ref, ref, z_send.at[k], z_recv.at[k], target))

    lanes = lax.broadcasted_iota(jnp.int32, (8, 128), 1)

    def padded(rows, filler):
        return jnp.concatenate(
            [rows, jnp.full((rows.shape[0], 128 - rows.shape[1]), filler, rows.dtype)], axis=1
        )

    def paired(rows):
        rows = padded(rows, -1)
        return jnp.where(lanes < 64, rows, pltpu.roll(pltpu.roll(rows, 4, 0), 64, 1))

    small_arrive(0, 3, 1)
    small_push(2, "a+", 3, 2, 1)
    small_arrive(1, 1, 1)
    push(0, 0, 1, "a+")
    push(0, 0, 0, "a-")
    own_past.wait()
    own_fit.wait()
    small_arrive(2, 2, 1)
    small_push(3, "b+", 0, 12, 4)
    small_push(4, "b-", 0, 4, 4)
    push(0, 0, 0, "b+")
    push(0, 0, 1, "b-")
    arrive(-1, 0, 0, "a+")
    arrive(1, 0, 1, "a-")
    own_w[0].wait()
    own_bi.wait()
    own_bo.wait()
    own_seeds.wait()
    multiply([(0, 0)], "first")
    small_arrive(3, 12, 4)
    small_push(5, "b+", 12, 8, 4)
    small_arrive(4, 4, 4)
    push(0, 0, 1, "b+")
    push(0, 0, 0, "b-")
    for da, h in ((-1, 0), (1, 1)):
        push(da, 0, h, "b+")
        push(da, 0, h, "b-")
    z_arrive(0, 1, 0, 4)
    z_relay(2, 1, 0, 4, up)
    z_arrive(4, 7, 0, 4)
    z_relay(5, 7, 0, 4, down)
    arrive(-1, 0, 1, "b+", "b-")
    arrive(1, 0, 0, "b+", "b-")
    arrive(0, -1, 0, "b+")
    arrive(0, 1, 1, "b-")
    z_arrive(2, 2, 0, 4)
    z_relay(3, 2, 0, 4, up)
    z_arrive(5, 6, 0, 4)
    z_relay(6, 6, 0, 4, down)
    small_arrive(5, 8, 4)
    go(remote(fit.at[0], fit.at[1], s_send.at[12], s_recv.at[12], sibling))
    multiply([(-1, 0), (1, 0)], "add")
    arrive(2, 0, 0, "b+", "b-")
    arrive(2, 0, 1, "b+", "b-")

    remote(fit.at[0], fit.at[1], s_send.at[12], s_recv.at[12], sibling).wait_recv()
    wide = lax.broadcasted_iota(jnp.int32, (16, 128), 1)
    mine, theirs = (
        padded(jnp.concatenate([fit[k, r] for r in range(16)], axis=0), FAR).astype(F32)
        for k in range(2)
    )
    everyone = jnp.where(wide < 64, mine, pltpu.roll(theirs, 64, 1))
    columns = jnp.concatenate([everyone, jnp.zeros((112, 128), F32)], axis=0).T
    packed = jnp.where(lanes < 64, mine[:8], pltpu.roll(mine[8:], 64, 1))
    sums = [jnp.zeros((8, 128), F32) for _ in range(8)]
    for j in range(16):
        column = jnp.broadcast_to(columns[:, j : j + 1], (128, 128))
        for m in range(8):
            sign = jnp.clip(packed[m : m + 1, :] - column, -1.0, 1.0)
            sums[m] += jnp.sum(sign.reshape(16, 8, 128), axis=0)
    ranks = jnp.concatenate([jnp.sum(s, axis=0, keepdims=True) for s in sums], axis=0) + 512.0
    turned = pltpu.roll(ranks, 64, 1)
    for first, low, high in ((0, ranks, turned), (8, turned, ranks)):
        both = jnp.where(lanes < 64, low, high)
        coarse = jnp.floor(both * (1.0 / 16.0)) * 16.0
        weights[0, first : first + 8] = coarse
        weights[1, first : first + 8] = both - coarse

    arrive(0, -1, 1)
    arrive(0, 1, 0)

    levels = lax.broadcasted_iota(jnp.int32, (128, 128), 0)

    def hot(rows):
        return [one_hot_row(levels, rows[j : j + 1]).astype(F32).astype(BF16) for j in range(4)]

    coup[...] = jnp.zeros_like(coup)

    def couple(first, last):
        @pl.loop(first, last)
        def _(r):
            coarse = weights[0, pl.ds(r, 1), :]
            fine = weights[1, pl.ds(r, 1), :]
            features = paired(past[0, r, 1])
            tops, rests = [], []
            for j in range(4):
                hit = one_hot_row(levels, features[j : j + 1])
                tops.append(jnp.where(hit, coarse, 0.0).astype(BF16))
                rests.append(jnp.where(hit, fine, 0.0).astype(BF16))
            lhs = jnp.concatenate(
                [jnp.concatenate(tops, axis=1), jnp.concatenate(rests, axis=1)], axis=0
            )
            coup[...] += nt(lhs, jnp.concatenate(hot(paired(past[0, r, 0])), axis=1))

    couple(0, 8)
    arrive(-1, -1, 0, "b+")
    arrive(-1, 1, 0)
    z_arrive(3, 3, 0, 4)
    z_half_up = z_block(bi, (z + DEPTH - 3) % DEPTH * 4, 2)
    go(remote(z_half_up, z_half_up, z_send.at[4], z_recv.at[1], up))
    z_arrive(6, 5, 0, 4)
    z_half_down = z_block(bi, (z + DEPTH - 5) % DEPTH * 4 + 2, 2)
    go(remote(z_half_down, z_half_down, z_send.at[7], z_recv.at[7], down))
    couple(8, 16)
    shares[0] = coup[:128, :] + coup[128:, :]
    multiply([(0, -1), (0, 1)], "add")
    go(remote(shares.at[0], shares.at[1], s_send.at[13], s_recv.at[13], sibling))
    arrive(1, -1, 1)
    arrive(1, 1, 1, "b-")
    z_arrive(1, 4, 0, 2)
    z_arrive(7, 4, 2, 2)

    for block in sorted(loads):
        loads.pop(block).wait()
    def project(g, total):
        lhs, rhs = [], []
        for db in range(RING):
            color = (c + g // RING) % 2
            lhs.append(tok[g * RING + db])
            rhs.append(bi[column_block(g % RING, db, color)])
        return total + nn(jnp.concatenate(lhs, axis=1), jnp.concatenate(rhs, axis=0))

    tokens = tok.shape[1]
    projected = lax.fori_loop(0, 2 * RING, project, jnp.zeros((tokens, 128), F32))
    p_high = projected.astype(BF16)
    arrive(-1, -1, 1)
    arrive(-1, 1, 1, "b-")
    remote(shares.at[0], shares.at[1], s_send.at[13], s_recv.at[13], sibling).wait_recv()
    coupling = ((shares[0] + shares[1]) * (STEP_SCALE / (2.0 * (16 * 96 - 1)))).T
    c_high, c_low = halves(coupling)
    own_in = bi[column_block(0, 0, c)]
    m_high, m_low = halves(nt(c_high, own_in) + nt(c_low, own_in))
    update = nn(jnp.concatenate([bo[...], bo[...]], axis=1), jnp.concatenate([m_high, m_low], axis=0))
    nw[...] = (w[0].astype(F32) + update).astype(BF16)
    arrive(1, -1, 0, "b+")
    arrive(1, 1, 0)
    multiply([(-1, -1), (-1, 1)], "add")
    arrive(0, 2, 0)
    arrive(0, 2, 1)
    multiply([(1, -1), (1, 1)], "add")
    outs, ins = hot(paired(seeds[0])), jnp.concatenate(hot(paired(seeds[1])), axis=1)
    picked = nn(p_high, ins)
    member = lax.shift_right_logical(lax.broadcasted_iota(jnp.int32, picked.shape, 0), 4)
    lane = lax.broadcasted_iota(jnp.int32, picked.shape, 1) & 63
    own_picks = jnp.where(member == lane, picked, 0.0).astype(BF16)
    term = NOISE_SCALE * nt(own_picks, jnp.concatenate(outs, axis=1)) + nt(
        jnp.concatenate([p_high, p_high], axis=1), jnp.concatenate([c_high, c_low], axis=1)
    )
    z_high, z_low = halves(term)
    zz[0] = z_high
    zz[1] = z_low
    arrive(2, -1, 0, "b+")
    arrive(2, 1, 0)
    arrive(2, -1, 1)
    arrive(2, 1, 1, "b-")
    multiply([(2, 0), (0, 2)], "term")
    arrive(-1, 2, 0)
    arrive(-1, 2, 1)
    multiply([(2, -1), (2, 1)], "add")
    arrive(1, 2, 0)
    arrive(1, 2, 1)
    arrive(2, 2, 0)
    arrive(2, 2, 1)
    multiply([(-1, 2), (1, 2)], "add")
    sib_arrive(2, 2)

    for copy in pending:
        copy.wait_send()


def finish(acc, w_last, tok_last, nw, hidden_hbm, nw_hbm, out, done):
    weights_out = pltpu.make_async_copy(nw, nw_hbm, done.at[2])
    weights_out.start()
    lhs = jnp.concatenate([tok_last[0], tok_last[1]], axis=1)
    first = out.shape[1] * 4 // 7
    copies = []
    for k, (start, size) in enumerate(((0, first), (first, out.shape[1] - first))):
        span = pl.ds(start, size)
        rhs = jnp.concatenate([w_last[0, span, :], w_last[1, span, :]], axis=1)
        out[:, span] = (acc[:, span] + nt(lhs, rhs)).astype(BF16)
        copies.append(pltpu.make_async_copy(out.at[:, span], hidden_hbm.at[:, span], done.at[k]))
        copies[-1].start()
    for copy in copies:
        copy.wait()
    weights_out.wait()


def shards(tokens, weight, bank_in, bank_out, fitness, past_seeds, new_seeds):
    members, each, features = tokens.shape
    rows, wide = weight.shape
    flat = members * each
    seeds = (*past_seeds.shape[1:], members)
    dma = pltpu.SemaphoreType.DMA
    parts = pl.pallas_call(
        kernel,
        out_shape=(
            pltpu.VMEM((flat, rows), F32),
            pltpu.VMEM((2, rows, 128), BF16),
            pltpu.VMEM((2, flat, 128), BF16),
            pltpu.VMEM((rows, wide), BF16),
        ),
        in_specs=[pl.BlockSpec(memory_space=pl.ANY)] * 7,
        out_specs=[pl.BlockSpec(memory_space=pltpu.VMEM)] * 4,
        scratch_shapes=[
            pltpu.VMEM((32, flat, 128), BF16),
            pltpu.VMEM((32, rows, 128), BF16),
            pltpu.VMEM((32, 128, 128), BF16),
            pltpu.VMEM((rows, 128), BF16),
            pltpu.VMEM((2, 16, *seeds), jnp.int32),
            pltpu.VMEM((2, 16, 1, members), jnp.int32),
            pltpu.VMEM(seeds, jnp.int32),
            pltpu.VMEM((2, 16, 128), F32),
            pltpu.VMEM((256, 128), F32),
            pltpu.VMEM((2, 128, 128), F32),
            pltpu.VMEM((2, flat, 128), BF16),
            dma((128,)), dma((32,)), dma((32,)), dma((32,)), dma((8,)), dma((8,)),
            dma((14,)), dma((14,)), dma((34,)), dma((6,)),
        ],
        compiler_params=pltpu.CompilerParams(
            collective_id=0, has_side_effects=True, vmem_limit_bytes=52 * 1024 * 1024
        ),
    )(
        tokens.reshape(flat, features), weight, bank_in.reshape(4, 128, 128), bank_out,
        fitness.reshape(1, members), past_seeds.transpose(1, 2, 0), new_seeds.transpose(1, 2, 0),
    )
    hidden, new_weight = pl.pallas_call(
        finish,
        out_shape=(
            jax.ShapeDtypeStruct((flat, rows), BF16),
            jax.ShapeDtypeStruct((rows, wide), BF16),
        ),
        in_specs=[pl.BlockSpec(memory_space=pltpu.VMEM)] * 4,
        out_specs=[pl.BlockSpec(memory_space=pl.ANY)] * 2,
        scratch_shapes=[pltpu.VMEM((flat, rows), BF16), dma((3,))],
        compiler_params=pltpu.CompilerParams(vmem_limit_bytes=32 * 1024 * 1024),
    )(*parts)
    return hidden.reshape(members, each, rows), new_weight


def solution(mesh):
    torus = Mesh(
        mesh.devices.reshape(4, 4, 2, mesh.shape["row"]), ("pop_0", "pop_1", "pop_2", "row")
    )
    return jax.shard_map(
        shards,
        mesh=torus,
        in_specs=(
            P(POP, None, None),
            P("row", POP),
            P("row", None),
            P("row", None),
            P(POP),
            P(POP, None, None),
            P(POP, None, None),
        ),
        out_specs=(P(POP, None, "row"), P("row", POP)),
        check_vma=False,
    )
```

```python
import functools

import jax
import jax.numpy as jnp
from jax import lax
from jax.experimental import pallas as pl
from jax.experimental.pallas import tpu as pltpu
from jax.sharding import Mesh
from jax.sharding import PartitionSpec as P

POP = ("pop_0", "pop_1", "pop_2")
MESH = pl.DeviceIdType.MESH

NOISE_SCALE = 0.1
STEP_SCALE = 0.03

RING = 4
DEPTH = 8
FAR = 1 << 20
F32 = jnp.float32
BF16 = jnp.bfloat16


def nt(a, b):
    return lax.dot_general(a, b, (((1,), (1,)), ((), ())), preferred_element_type=F32)


def nn(a, b):
    return jnp.dot(a, b, preferred_element_type=F32)


def halves(a):
    high = a.astype(BF16)
    return high, (a - high.astype(F32)).astype(BF16)


def slot(da, db):
    return (da % RING) * RING + db % RING


LAST = (slot(2, 2), 16 + slot(2, 2))


def one_hot_row(levels, row):
    return levels == jnp.broadcast_to(row, levels.shape)


def kernel(
    tok_hbm, w_hbm, bi_hbm, bo_hbm, fit_hbm, past_hbm, seeds_hbm,
    acc, w_last, tok_last, nw,
    tok, w, bi, bo, past, fit, seeds, weights, coup, shares, zz,
    send, recv, sib_send, sib_recv, z_send, z_recv, s_send, s_recv, tok_sem, local,
):
    x, y, c, z = (lax.axis_index(name) for name in (*POP, "row"))
    rows = w_hbm.shape[0]
    half = rows // 2
    other = 1 - c

    def place(da, db, color):
        px = (x + da * (1 - color) + db * color) % RING
        py = (y + da * color + db * (1 - color)) % RING
        return px, py

    def column_block(da, db, color):
        px, py = place(da, db, color)
        return (px * RING + py) * 2 + color

    def peer(da, db):
        px, py = place(da % RING, db % RING, c)
        return (px, py, c, z)

    ways = {"a+": (1, 0), "a-": (-1, 0), "b+": (0, 1), "b-": (0, -1)}
    sibling = (x, y, other, z)
    up, down = (x, y, c, (z + 1) % DEPTH), (x, y, c, (z + DEPTH - 1) % DEPTH)
    neighbours = [peer(*step) for step in ways.values()] + [sibling, up, down]

    barrier = pltpu.get_barrier_semaphore()
    for neighbour in neighbours:
        pl.semaphore_signal(barrier, inc=1, device_id=neighbour, device_id_type=MESH)
    pl.semaphore_wait(barrier, len(neighbours))

    pending = []

    def remote(src, dst, send_sem, recv_sem, target):
        return pltpu.make_async_remote_copy(
            src_ref=src, dst_ref=dst, send_sem=send_sem, recv_sem=recv_sem,
            device_id=target, device_id_type=MESH,
        )

    def go(copy):
        copy.start()
        pending.append(copy)

    def part(index, h):
        block = w_last.at[index // 16] if index in LAST else w.at[index]
        return block.at[pl.ds(h * half, half), :]

    order = {name: place_at for place_at, name in enumerate(ways)}

    def push(da, db, h, way):
        step = ways[way]
        there = slot(da - step[0], db - step[1])
        here = slot(da, db)
        source = w_hbm.at[pl.ds(h * half, half), :] if here == 0 else part(here, h)
        go(remote(source, part(there, h), send.at[order[way] * 32 + here * 2 + h],
                  recv.at[there * 2 + h], peer(*step)))

    def across(da, db, h):
        here = slot(da, db)
        source = w_hbm.at[pl.ds(h * half, half), :] if here == 0 else part(here, h)
        go(remote(source, part(16 + here, h), sib_send.at[here * 2 + h],
                  sib_recv.at[here * 2 + h], sibling))

    def arrive(da, db, h, *onward):
        here = slot(da, db)
        ref = part(here, h)
        remote(ref, ref, send.at[0], recv.at[here * 2 + h], sibling).wait_recv()
        for way in onward:
            push(da, db, h, way)
        across(da, db, h)

    def sib_arrive(da, db):
        here = slot(da, db)
        for h in range(2):
            ref = part(16 + here, h)
            remote(ref, ref, send.at[0], sib_recv.at[here * 2 + h], sibling).wait_recv()

    def small_push(k, way, first, there, count):
        for j, (ref, own) in enumerate(((past, past_hbm), (fit, fit_hbm))):
            if count == 1:
                source = own if first == 0 else ref.at[0, first]
                target = ref.at[0, there]
            else:
                source = ref.at[0, pl.ds(first, count)]
                target = ref.at[0, pl.ds(there, count)]
            go(remote(source, target, s_send.at[2 * k + j], s_recv.at[2 * k + j],
                      peer(*ways[way])))

    def small_arrive(k, there, count):
        for j, ref in enumerate((past, fit)):
            ref = ref.at[0, there] if count == 1 else ref.at[0, pl.ds(there, count)]
            remote(ref, ref, s_send.at[0], s_recv.at[2 * k + j], sibling).wait_recv()

    small_push(0, "a+", 0, 3, 1)
    small_push(1, "a-", 0, 1, 1)
    push(0, 0, 0, "a+")
    push(0, 0, 1, "a-")

    own_w = [pltpu.make_async_copy(w_hbm, w.at[0], local.at[0])]
    own_w[0].start()
    across(0, 0, 0)
    across(0, 0, 1)

    def z_block(ref, first, count):
        return ref.at[pl.ds(first, count)]

    z_own = z_block(bi, z * 4, 4)
    go(remote(bi_hbm, z_own, z_send.at[0], z_recv.at[0], up))
    go(remote(bi_hbm, z_own, z_send.at[1], z_recv.at[4], down))
    own_bi = pltpu.make_async_copy(bi_hbm, z_own, local.at[1])
    own_bi.start()
    own_past = pltpu.make_async_copy(past_hbm, past.at[0, 0], local.at[2])
    own_past.start()
    own_fit = pltpu.make_async_copy(fit_hbm, fit.at[0, 0], local.at[5])
    own_fit.start()
    own_bo = pltpu.make_async_copy(bo_hbm, bo, local.at[3])
    own_bo.start()
    own_seeds = pltpu.make_async_copy(seeds_hbm, seeds, local.at[4])
    own_seeds.start()

    loads = {}
    for color, at in ((c, 0), (other, 16)):
        for da in range(RING):
            for db in range(RING):
                start = pl.multiple_of(column_block(da, db, color) * 128, 128)
                index = at + slot(da, db)
                loads[index] = pltpu.make_async_copy(
                    tok_hbm.at[:, pl.ds(start, 128)], tok.at[index], tok_sem.at[index]
                )
                if index in LAST:
                    loads[32 + index // 16] = pltpu.make_async_copy(
                        tok_hbm.at[:, pl.ds(start, 128)],
                        tok_last.at[index // 16],
                        tok_sem.at[32 + index // 16],
                    )
    sequence = [(0, 0), (-1, 0), (1, 0), (0, -1), (0, 1), (2, 0), (0, 2), (-1, -1), (-1, 1),
                (1, -1), (1, 1), (2, -1), (2, 1), (-1, 2), (1, 2), (2, 2)]
    for place_at in sequence:
        for at in (0, 16):
            loads[at + slot(*place_at)].start()
    loads[32].start()
    loads[33].start()

    def blocks_of(places):
        return [at + slot(*place_at) for place_at in places for at in (0, 16)]

    def multiply(places, mode):
        blocks = blocks_of(places)
        for place_at in places:
            sib_arrive(*place_at)
        for block in blocks:
            if block in loads:
                loads.pop(block).wait()
        lhs = [tok[block] for block in blocks]
        extra = mode == "term"
        if extra:
            lhs += [zz[0], zz[1]]
        lhs = jnp.concatenate(lhs, axis=1)

        rhs = [w[block] for block in blocks]
        if extra:
            rhs += [bo[...], bo[...]]
        product = nt(lhs, jnp.concatenate(rhs, axis=1))
        if mode == "first":
            acc[...] = product
        else:
            acc[...] += product

    def z_arrive(k, behind, first, count):
        block = (z + DEPTH - behind) % DEPTH * 4 + first
        ref = z_block(bi, block, count)
        remote(ref, ref, z_send.at[0], z_recv.at[k], sibling).wait_recv()

    def z_relay(k, behind, first, count, target):
        block = (z + DEPTH - behind) % DEPTH * 4 + first
        ref = z_block(bi, block, count)
        go(remote(ref, ref, z_send.at[k], z_recv.at[k], target))

    lanes = lax.broadcasted_iota(jnp.int32, (8, 128), 1)

    def padded(rows, filler):
        return jnp.concatenate(
            [rows, jnp.full((rows.shape[0], 128 - rows.shape[1]), filler, rows.dtype)], axis=1
        )

    def paired(rows):
        rows = padded(rows, -1)
        return jnp.where(lanes < 64, rows, pltpu.roll(pltpu.roll(rows, 4, 0), 64, 1))

    small_arrive(0, 3, 1)
    small_push(2, "a+", 3, 2, 1)
    small_arrive(1, 1, 1)
    push(0, 0, 1, "a+")
    push(0, 0, 0, "a-")
    own_past.wait()
    own_fit.wait()
    small_arrive(2, 2, 1)
    small_push(3, "b+", 0, 12, 4)
    small_push(4, "b-", 0, 4, 4)
    push(0, 0, 0, "b+")
    push(0, 0, 1, "b-")
    arrive(-1, 0, 0, "a+")
    arrive(1, 0, 1, "a-")
    own_w[0].wait()
    own_bi.wait()
    own_bo.wait()
    own_seeds.wait()
    multiply([(0, 0)], "first")
    small_arrive(3, 12, 4)
    small_push(5, "b+", 12, 8, 4)
    small_arrive(4, 4, 4)
    push(0, 0, 1, "b+")
    push(0, 0, 0, "b-")
    for da, h in ((-1, 0), (1, 1)):
        push(da, 0, h, "b+")
        push(da, 0, h, "b-")
    z_arrive(0, 1, 0, 4)
    z_relay(2, 1, 0, 4, up)
    z_arrive(4, 7, 0, 4)
    z_relay(5, 7, 0, 4, down)
    arrive(-1, 0, 1, "b+", "b-")
    arrive(1, 0, 0, "b+", "b-")
    arrive(0, -1, 0, "b+")
    arrive(0, 1, 1, "b-")
    z_arrive(2, 2, 0, 4)
    z_relay(3, 2, 0, 4, up)
    z_arrive(5, 6, 0, 4)
    z_relay(6, 6, 0, 4, down)
    small_arrive(5, 8, 4)
    go(remote(fit.at[0], fit.at[1], s_send.at[12], s_recv.at[12], sibling))
    multiply([(-1, 0), (1, 0)], "add")
    arrive(2, 0, 0, "b+", "b-")
    arrive(2, 0, 1, "b+", "b-")

    remote(fit.at[0], fit.at[1], s_send.at[12], s_recv.at[12], sibling).wait_recv()
    wide = lax.broadcasted_iota(jnp.int32, (16, 128), 1)
    mine, theirs = (
        padded(jnp.concatenate([fit[k, r] for r in range(16)], axis=0), FAR).astype(F32)
        for k in range(2)
    )
    everyone = jnp.where(wide < 64, mine, pltpu.roll(theirs, 64, 1))
    columns = jnp.concatenate([everyone, jnp.zeros((112, 128), F32)], axis=0).T
    packed = jnp.where(lanes < 64, mine[:8], pltpu.roll(mine[8:], 64, 1))
    sums = [jnp.zeros((8, 128), F32) for _ in range(8)]
    for j in range(16):
        column = jnp.broadcast_to(columns[:, j : j + 1], (128, 128))
        for m in range(8):
            sign = jnp.clip(packed[m : m + 1, :] - column, -1.0, 1.0)
            sums[m] += jnp.sum(sign.reshape(16, 8, 128), axis=0)
    ranks = jnp.concatenate([jnp.sum(s, axis=0, keepdims=True) for s in sums], axis=0) + 512.0
    turned = pltpu.roll(ranks, 64, 1)
    for first, low, high in ((0, ranks, turned), (8, turned, ranks)):
        both = jnp.where(lanes < 64, low, high)
        coarse = jnp.floor(both * (1.0 / 16.0)) * 16.0
        weights[0, first : first + 8] = coarse
        weights[1, first : first + 8] = both - coarse

    arrive(0, -1, 1)
    arrive(0, 1, 0)

    levels = lax.broadcasted_iota(jnp.int32, (128, 128), 0)

    def hot(rows):
        return [one_hot_row(levels, rows[j : j + 1]).astype(F32).astype(BF16) for j in range(4)]

    coup[...] = jnp.zeros_like(coup)

    def couple(first, last):
        @pl.loop(first, last)
        def _(r):
            coarse = weights[0, pl.ds(r, 1), :]
            fine = weights[1, pl.ds(r, 1), :]
            features = paired(past[0, r, 1])
            tops, rests = [], []
            for j in range(4):
                hit = one_hot_row(levels, features[j : j + 1])
                tops.append(jnp.where(hit, coarse, 0.0).astype(BF16))
                rests.append(jnp.where(hit, fine, 0.0).astype(BF16))
            lhs = jnp.concatenate(
                [jnp.concatenate(tops, axis=1), jnp.concatenate(rests, axis=1)], axis=0
            )
            coup[...] += nt(lhs, jnp.concatenate(hot(paired(past[0, r, 0])), axis=1))

    couple(0, 8)
    arrive(-1, -1, 0, "b+")
    arrive(-1, 1, 0)
    z_arrive(3, 3, 0, 4)
    z_half_up = z_block(bi, (z + DEPTH - 3) % DEPTH * 4, 2)
    go(remote(z_half_up, z_half_up, z_send.at[4], z_recv.at[1], up))
    z_arrive(6, 5, 0, 4)
    z_half_down = z_block(bi, (z + DEPTH - 5) % DEPTH * 4 + 2, 2)
    go(remote(z_half_down, z_half_down, z_send.at[7], z_recv.at[7], down))
    couple(8, 16)
    shares[0] = coup[:128, :] + coup[128:, :]
    multiply([(0, -1), (0, 1)], "add")
    go(remote(shares.at[0], shares.at[1], s_send.at[13], s_recv.at[13], sibling))
    arrive(1, -1, 1)
    arrive(1, 1, 1, "b-")
    z_arrive(1, 4, 0, 2)
    z_arrive(7, 4, 2, 2)

    for block in sorted(loads):
        loads.pop(block).wait()
    def project(g, total):
        lhs, rhs = [], []
        for db in range(RING):
            color = (c + g // RING) % 2
            lhs.append(tok[g * RING + db])
            rhs.append(bi[column_block(g % RING, db, color)])
        return total + nn(jnp.concatenate(lhs, axis=1), jnp.concatenate(rhs, axis=0))

    tokens = tok.shape[1]
    projected = lax.fori_loop(0, 2 * RING, project, jnp.zeros((tokens, 128), F32))
    p_high = projected.astype(BF16)
    arrive(-1, -1, 1)
    arrive(-1, 1, 1, "b-")
    remote(shares.at[0], shares.at[1], s_send.at[13], s_recv.at[13], sibling).wait_recv()
    coupling = ((shares[0] + shares[1]) * (STEP_SCALE / (2.0 * (16 * 96 - 1)))).T
    c_high, c_low = halves(coupling)
    own_in = bi[column_block(0, 0, c)]
    m_high, m_low = halves(nt(c_high, own_in) + nt(c_low, own_in))
    update = nn(jnp.concatenate([bo[...], bo[...]], axis=1), jnp.concatenate([m_high, m_low], axis=0))
    nw[...] = (w[0].astype(F32) + update).astype(BF16)
    arrive(1, -1, 0, "b+")
    arrive(1, 1, 0)
    multiply([(-1, -1), (-1, 1)], "add")
    arrive(0, 2, 0)
    arrive(0, 2, 1)
    multiply([(1, -1), (1, 1)], "add")
    outs, ins = hot(paired(seeds[0])), jnp.concatenate(hot(paired(seeds[1])), axis=1)
    picked = nn(p_high, ins)
    member = lax.shift_right_logical(lax.broadcasted_iota(jnp.int32, picked.shape, 0), 4)
    lane = lax.broadcasted_iota(jnp.int32, picked.shape, 1) & 63
    own_picks = jnp.where(member == lane, picked, 0.0).astype(BF16)
    term = NOISE_SCALE * nt(own_picks, jnp.concatenate(outs, axis=1)) + nt(
        jnp.concatenate([p_high, p_high], axis=1), jnp.concatenate([c_high, c_low], axis=1)
    )
    z_high, z_low = halves(term)
    zz[0] = z_high
    zz[1] = z_low
    arrive(2, -1, 0, "b+")
    arrive(2, 1, 0)
    arrive(2, -1, 1)
    arrive(2, 1, 1, "b-")
    multiply([(2, 0), (0, 2)], "term")
    arrive(-1, 2, 0)
    arrive(-1, 2, 1)
    arrive(1, 2, 0)
    arrive(1, 2, 1)
    multiply([(2, -1), (2, 1)], "add")
    arrive(2, 2, 0)
    arrive(2, 2, 1)
    multiply([(-1, 2), (1, 2)], "add")
    sib_arrive(2, 2)

    for copy in pending:
        copy.wait_send()


def finish(acc, w_last, tok_last, nw, hidden_hbm, nw_hbm, out, done):
    weights_out = pltpu.make_async_copy(nw, nw_hbm, done.at[4])
    weights_out.start()
    lhs = jnp.concatenate([tok_last[0], tok_last[1]], axis=1)
    wide = out.shape[1]
    copies = []
    for k, start in enumerate(range(0, wide, 512)):
        span = pl.ds(start, min(512, wide - start))
        rhs = jnp.concatenate([w_last[0, span, :], w_last[1, span, :]], axis=1)
        out[:, span] = (acc[:, span] + nt(lhs, rhs)).astype(BF16)
        copies.append(pltpu.make_async_copy(out.at[:, span], hidden_hbm.at[:, span], done.at[k]))
        copies[-1].start()
    for copy in copies:
        copy.wait()
    weights_out.wait()


def shards(tokens, weight, bank_in, bank_out, fitness, past_seeds, new_seeds):
    members, each, features = tokens.shape
    rows, wide = weight.shape
    flat = members * each
    seeds = (*past_seeds.shape[1:], members)
    dma = pltpu.SemaphoreType.DMA
    parts = pl.pallas_call(
        kernel,
        out_shape=(
            pltpu.VMEM((flat, rows), F32),
            pltpu.VMEM((2, rows, 128), BF16),
            pltpu.VMEM((2, flat, 128), BF16),
            pltpu.VMEM((rows, wide), BF16),
        ),
        in_specs=[pl.BlockSpec(memory_space=pl.ANY)] * 7,
        out_specs=[pl.BlockSpec(memory_space=pltpu.VMEM)] * 4,
        scratch_shapes=[
            pltpu.VMEM((32, flat, 128), BF16),
            pltpu.VMEM((32, rows, 128), BF16),
            pltpu.VMEM((32, 128, 128), BF16),
            pltpu.VMEM((rows, 128), BF16),
            pltpu.VMEM((2, 16, *seeds), jnp.int32),
            pltpu.VMEM((2, 16, 1, members), jnp.int32),
            pltpu.VMEM(seeds, jnp.int32),
            pltpu.VMEM((2, 16, 128), F32),
            pltpu.VMEM((256, 128), F32),
            pltpu.VMEM((2, 128, 128), F32),
            pltpu.VMEM((2, flat, 128), BF16),
            dma((128,)), dma((32,)), dma((32,)), dma((32,)), dma((8,)), dma((8,)),
            dma((14,)), dma((14,)), dma((34,)), dma((6,)),
        ],
        compiler_params=pltpu.CompilerParams(
            collective_id=0, has_side_effects=True, vmem_limit_bytes=52 * 1024 * 1024
        ),
    )(
        tokens.reshape(flat, features), weight, bank_in.reshape(4, 128, 128), bank_out,
        fitness.reshape(1, members), past_seeds.transpose(1, 2, 0), new_seeds.transpose(1, 2, 0),
    )
    hidden, new_weight = pl.pallas_call(
        finish,
        out_shape=(
            jax.ShapeDtypeStruct((flat, rows), BF16),
            jax.ShapeDtypeStruct((rows, wide), BF16),
        ),
        in_specs=[pl.BlockSpec(memory_space=pltpu.VMEM)] * 4,
        out_specs=[pl.BlockSpec(memory_space=pl.ANY)] * 2,
        scratch_shapes=[pltpu.VMEM((flat, rows), BF16), dma((5,))],
        compiler_params=pltpu.CompilerParams(vmem_limit_bytes=32 * 1024 * 1024),
    )(*parts)
    return hidden.reshape(members, each, rows), new_weight


def solution(mesh):
    torus = Mesh(
        mesh.devices.reshape(4, 4, 2, mesh.shape["row"]), ("pop_0", "pop_1", "pop_2", "row")
    )
    return jax.shard_map(
        shards,
        mesh=torus,
        in_specs=(
            P(POP, None, None),
            P("row", POP),
            P("row", None),
            P("row", None),
            P(POP),
            P(POP, None, None),
            P(POP, None, None),
        ),
        out_specs=(P(POP, None, "row"), P("row", POP)),
        check_vma=False,
    )
```
